256 devices in a mesh: grp: 8 (over z), gx: 8 (over y, core), gy: 4 (over x).
Axes of the slice: x: 4, y: 4, z: 8, core: 2. Of those that a mesh axis runs over, the one named last changes fastest.
Arguments:
- fluid_state: bfloat16 [8, 4, 125, 8, 8, 128], P('grp', None, None, 'gx', 'gy'), may hold values from -6 to 6
- mesh_velocity: bfloat16 [8, 3, 125, 8, 8, 128], P('grp', None, None, 'gx', 'gy'), may hold values from -3 to 3
- metric: float32 [8, 3, 8, 8, 128], P('grp', None, 'gx', 'gy'), may hold values from 0.5 to 2
- wall_face: int32 [65536], P(('grp', 'gx', 'gy')), may hold values from 1 to 510, as said below
- wall_owner: int32 [65536, 1], P(('grp', 'gx', 'gy')), may hold values from 0 to 31; in each aligned block of 256 rows (0 to 255, 256 to 511, ...) at most 16 rows name the same one
- wall_target: int32 [65536], P(('grp', 'gx', 'gy')), may hold values from 0 to 4095
- solid_disp: float32 [8, 81, 131072], P('grp', None, ('gx', 'gy')), may hold values from -6 to 6
- modulus: float32 [8, 131072], P('grp', ('gx', 'gy')), may hold values from 0.5 to 4
- stiffness: float32 [81, 81], replicated, may hold values from -0.011 to 2, as said below
Outputs:
- fluid_next: bfloat16 [8, 4, 125, 8, 8, 128], P('grp', None, None, 'gx', 'gy')
- mesh_motion: bfloat16 [8, 6, 125, 8, 8, 128], P('grp', None, None, 'gx', 'gy')
- solid_next: float32 [8, 81, 131072], P('grp', None, ('gx', 'gy'))
The draws below stay inside these ranges and needn't reach their ends.
Inputs may be any that keep to these rules, and one draw needn't show every extreme that they name: `wall_face`: within the rows of one device the ids are distinct; ids below 256 are lower z faces, the others upper z faces of element id - 256. Walls lie between neighbouring elements of a device along z: the upper face of an element is listed exactly when the lower face of the next element along z is listed; outer z faces of the grid are never listed. `wall_owner`: the owner is the device of this column (gx * size of gy + gy) in solid group 6 + (g mod 2) for a row of fluid group g. Within the rows of one device at most 16 rows name one column, and some column has exactly 16. `wall_target`: A solid element of the owner's block of 4096. `stiffness`: diagonal entries lie in 1 to 2; the off-diagonal entries of a row sum in magnitude to less than 0.9.
All inputs are finite; a program needn't handle non-finite values.
Results may differ from the reference program's by a relative error of at most 0.001.
Values sent between devices are 32-bit elements; how exact they have to be, the bound alone decides.
A program may use at most 128 MiB of HBM per device.

```python
import math
import jax
import jax.numpy as jnp
import numpy as np
from jax import lax

FIELDS = 4
FLUID_NODES = 125
SOLID_NODES = 27
BX = 1
BY = 2
BZ = 128
WALL = 256
SE = 4096
SWEEPS = 4
ELEMS = 256
CAP = 16
NXE = 8
NYE = 8
WALL_ALL = 65536
SE_ALL = 131072
N_GRP = 8
N_GX = 8
N_GY = 4


def draw_wall_face(key, part):
    block_count = WALL_ALL // WALL
    block_keys = jax.random.split(jax.random.fold_in(key, 3), block_count)
    interfaces = BX * BY * (BZ - 1)

    def one_block(block_key):
        chosen = jax.random.permutation(block_key, interfaces)[:WALL // 2]
        element = chosen // (BZ - 1) * BZ + chosen % (BZ - 1)
        return jnp.stack([ELEMS + element, element + 1], 1).reshape(WALL)
    return jax.vmap(one_block)(block_keys).reshape(WALL_ALL).astype(jnp.int32)


def draw_stiffness(key, part):
    first_key = jax.random.fold_in(key, 11)
    second_key = jax.random.fold_in(key, 12)
    diagonal = jax.random.uniform(first_key, (81,), jnp.float32, 1.0, 2.0)
    coupling = jax.random.uniform(second_key, (81, 81), jnp.float32, -0.011, 0.011)
    identity = jnp.eye(81, dtype=jnp.float32)
    return coupling * (1.0 - identity) + identity * diagonal[None, :]


def with_ends(values, rng, smallest, largest):
    longest = values.shape.index(max(values.shape))
    spots = []
    for shift in (0, 1):
        where = [jax.random.randint(jax.random.fold_in(rng, axis), (), 0, length) for axis, length in enumerate(values.shape)]
        where[longest] = (where[longest] + shift) % values.shape[longest]
        spots.append(tuple(where))
    return values.at[spots[0]].set(smallest).at[spots[1]].set(largest)


def block_levels(key, extent, cuts, low, high):
    gain, own = 1.0, jax.random.fold_in(key, 6)
    for axis_at, blocks in cuts:
        steps = jnp.exp(jax.random.uniform(jax.random.fold_in(own, axis_at), (blocks,), jnp.float32, low / len(cuts), high / len(cuts)))
        gain = gain * jnp.repeat(steps, extent[axis_at] // blocks).reshape([-1 if axis == axis_at else 1 for axis in range(len(extent))])
    return gain


def shared_out(stream_key, own, number, rows, number_of, top, most, slope):
    order = jax.random.permutation(stream_key, number_of)
    packed, common = load_shares(number_of, rows * top, most, slope, True), load_shares(number_of, rows * top, most, slope, False)
    places = jnp.arange(number_of)

    def named(tallies, rotation):
        used = int((tallies > 0).sum())
        fixed = max(1, used // 4)
        shifted = fixed + (places - fixed + rotation * (used - fixed)) % max(1, number_of - fixed)
        return jnp.zeros((number_of,), jnp.int32).at[order[jnp.where(places < fixed, places, shifted)]].set(jnp.asarray(tallies, jnp.int32))

    tallies = jnp.where(number % 4 == 0, named(packed, number // 4), named(common, number - number // 4 - 1))
    mixed = jax.random.permutation(jax.random.fold_in(own, 3), number_of)
    giver, taker = mixed[0:number_of // 2 * 2:2], mixed[1:number_of // 2 * 2:2]
    slack = jnp.minimum(tallies[giver] - 1, most - tallies[taker]) // 2
    slack = jnp.where((giver == order[0]) | (taker == order[0]) | (tallies[taker] == 0), 0, jnp.maximum(slack, 0))
    shifted = jax.random.randint(jax.random.fold_in(own, 4), (number_of // 2,), 0, 1 << 20) % (slack + 1)
    tallies = tallies.at[giver].add(-shifted).at[taker].add(shifted)
    members = jnp.searchsorted(jnp.cumsum(tallies), jnp.arange(rows * top), side="right").astype(jnp.int32)
    listing = members.reshape(top, rows).T
    listing = listing[jax.random.permutation(jax.random.fold_in(own, 1), rows)]
    rotation = jax.random.randint(jax.random.fold_in(own, 2), (rows, 1), 0, top)
    return jnp.take_along_axis(listing, (jnp.arange(top)[None, :] + rotation) % top, axis=1)


def load_shares(number_of, total, reach, skew, full):
    loads = [(1 << 20) // math.isqrt(rank ** skew) + 1 for rank in range(1, number_of + 1)]
    largest = reach if full else min(reach, max(-(-total // number_of), total * loads[0] // sum(loads)))
    least = 1 if total - largest >= number_of - 1 else 0
    holding, surplus = [largest] + [least] * (number_of - 1), total - largest - least * (number_of - 1)
    while surplus > 0:
        free = [i for i in range(1, number_of) if holding[i] < largest] or [i for i in range(1, number_of) if holding[i] < reach]
        pool, budget = sum([loads[i] for i in free]), surplus
        for i in free:
            addition = min(reach - holding[i], max(1, budget * loads[i] // pool), surplus)
            holding[i] = holding[i] + addition
            surplus = surplus - addition
    return np.array(holding)


def noise(stream_key, dims, deviation, bound, cuts=(), kind=jnp.bfloat16):
    entries = deviation * jax.random.normal(stream_key, dims, jnp.float32)
    if cuts:
        entries = entries * block_levels(stream_key, dims, cuts, -0.22, 0.18)
    return jnp.clip(entries, -bound, bound).astype(kind)


def setup_inputs(seed: int = 0) -> dict:
    streams_of = jax.random.split(jax.random.key(seed), 10)
    fluid_state = noise(streams_of[0], (N_GRP, FIELDS, FLUID_NODES, NXE, NYE, BZ), 1.0, 6.0, ((0, 8), (3, 8), (4, 4)))
    mesh_velocity = noise(streams_of[1], (N_GRP, 3, FLUID_NODES, NXE, NYE, BZ), 0.5, 3.0, ((0, 8), (3, 8), (4, 4)))
    metric = jnp.clip(jnp.exp(math.log(2.0) - 1.3862944 * jax.random.uniform(streams_of[2], (N_GRP, 3, NXE, NYE, BZ), jnp.float32) ** block_levels(streams_of[2], (N_GRP, 3, NXE, NYE, BZ), ((0, 8), (2, 8), (3, 4)), -0.2, 0.2)), 0.5, 2.0)
    wall_face = draw_wall_face(jax.random.fold_in(streams_of[9], 71), 0)
    wall_owner_keys = jax.random.split(jax.random.fold_in(streams_of[4], 1), WALL_ALL // WALL)
    wall_owner_turns = jax.random.permutation(jax.random.fold_in(streams_of[4], 3), WALL_ALL // WALL)
    wall_owner = jax.vmap(lambda own, number: shared_out(jax.random.fold_in(streams_of[4], 2), own, number, WALL, N_GX * N_GY, 1, CAP, 2))(wall_owner_keys, wall_owner_turns).reshape((WALL_ALL, 1))
    wall_target = with_ends(jax.random.randint(streams_of[5], (WALL_ALL,), 0, SE), jax.random.fold_in(streams_of[5], 1), 0, SE - 1).astype(jnp.int32)
    solid_disp = noise(streams_of[6], (N_GRP, 3 * SOLID_NODES, SE_ALL), 1.0, 6.0, ((0, 8), (2, 32)), jnp.float32)
    modulus = jnp.clip(jnp.exp(math.log(4.0) - 2.0794415 * jax.random.uniform(streams_of[7], (N_GRP, SE_ALL), jnp.float32) ** block_levels(streams_of[7], (N_GRP, SE_ALL), ((0, 8), (1, 32)), -0.2, 0.2)), 0.5, 4.0)
    stiffness = draw_stiffness(jax.random.fold_in(streams_of[9], 71), 0)
    return dict(fluid_state=fluid_state, mesh_velocity=mesh_velocity, metric=metric, wall_face=wall_face, wall_owner=wall_owner, wall_target=wall_target, solid_disp=solid_disp, modulus=modulus, stiffness=stiffness)


viscosity = 0.02
penalty = 2.0
time_step = 0.05
traction_scale = 0.2
mismatch_gain = 0.5
relaxation = 0.8

def fluid_points():
    return np.array([-1.0, -math.sqrt(3.0 / 7.0), 0.0, math.sqrt(3.0 / 7.0), 1.0])

def fluid_weights():
    return np.array([0.1, 49.0 / 90.0, 32.0 / 45.0, 49.0 / 90.0, 0.1])

def lagrange_table(centres, points):
    result = np.ones((len(points), len(centres)))
    for column in range(len(centres)):
        for partner in range(len(centres)):
            if partner != column:
                result[:, column] = result[:, column] * (points - centres[partner]) / (centres[column] - centres[partner])
    return result

def derivative_table():
    points = fluid_points()
    length = len(points)
    weights = np.ones(length)
    for column in range(length):
        for partner in range(length):
            if partner != column:
                weights[column] = weights[column] / (points[column] - points[partner])
    result = np.zeros((length, length))
    for position in range(length):
        for column in range(length):
            if position != column:
                result[position, column] = weights[column] / weights[position] / (points[position] - points[column])
        result[position, position] = -np.sum(result[position])
    return jnp.asarray(result, jnp.float32)

def face_tables():
    values = lagrange_table(np.array([-1.0, 0.0, 1.0]), fluid_points())
    project_one = (values * fluid_weights()[:, None]).T
    return (jnp.asarray(np.kron(project_one, project_one), jnp.float32), jnp.asarray(np.kron(values, values), jnp.float32))

def derive_along(matrix, fields, direction):
    patterns = ('ia,fajkxyz->fijkxyz', 'ja,fiakxyz->fijkxyz', 'ka,fijaxyz->fijkxyz')
    return jnp.einsum(patterns[direction], matrix, fields, precision=lax.Precision.HIGHEST)

def volume_terms(fields, mesh_speed, metric, matrix):
    gradient = [metric[direction] * derive_along(matrix, fields, direction) for direction in range(3)]
    advect = sum(((fields[direction] - mesh_speed[direction]) * gradient[direction][0:3] for direction in range(3)))
    second = sum((metric[direction] * derive_along(matrix, gradient[direction][0:3], direction) for direction in range(3)))
    pressure_grad = jnp.stack([gradient[direction][3] for direction in range(3)])
    momentum = viscosity * second - advect - pressure_grad
    continuity = -(gradient[0][0] + gradient[1][1] + gradient[2][2])
    return (jnp.concatenate([momentum, continuity[None]], 0), gradient)

def edge_shape(fields, direction):
    shape_list = list(fields.shape)
    shape_list[direction + 1] = 1
    shape_list[direction + 4] = 1
    return tuple(shape_list)

def zero_side(fields, direction):
    zeroed = jnp.zeros(edge_shape(fields, direction), jnp.float32)
    return (zeroed, zeroed)

def face_update(fields, slopes, direction, lower_side, upper_side, open_low=1.0, open_high=1.0):
    node_axis = direction + 1
    cell_axis = direction + 4
    length = fields.shape[cell_axis]
    low_value = lax.index_in_dim(fields, 0, node_axis, True)
    high_value = lax.index_in_dim(fields, 4, node_axis, True)
    low_slope = lax.index_in_dim(slopes, 0, node_axis, True)
    high_slope = lax.index_in_dim(slopes, 4, node_axis, True)
    prev_value = jnp.concatenate([lower_side[0], lax.slice_in_dim(high_value, 0, length - 1, axis=cell_axis)], cell_axis) * open_low
    prev_slope = jnp.concatenate([lower_side[1], lax.slice_in_dim(high_slope, 0, length - 1, axis=cell_axis)], cell_axis) * open_low
    next_value = jnp.concatenate([lax.slice_in_dim(low_value, 1, length, axis=cell_axis), upper_side[0]], cell_axis) * open_high
    next_slope = jnp.concatenate([lax.slice_in_dim(low_slope, 1, length, axis=cell_axis), upper_side[1]], cell_axis) * open_high
    add_high = 0.5 * (next_slope - high_slope) + penalty * (next_value - high_value)
    add_low = 0.5 * (low_slope - prev_slope) - penalty * (low_value - prev_value)
    middle = jnp.zeros_like(lax.slice_in_dim(fields, 1, 4, axis=node_axis))
    return jnp.concatenate([add_low, middle, add_high], node_axis)

def rate_terms(fields, mesh_speed, metric, matrix, open_low, open_high):
    changes, gradient = volume_terms(fields, mesh_speed, metric, matrix)
    for direction in range(2):
        changes = changes + face_update(fields, gradient[direction], direction, zero_side(fields, direction), zero_side(fields, direction))
    changes = changes + face_update(fields, gradient[2], 2, zero_side(fields, 2), zero_side(fields, 2), open_low, open_high)
    return (changes, gradient)

def wall_blocks(fields, mesh_speed, slopes_z):
    both_sides = []
    for node_layer, normal in ((0, -1.0), (4, 1.0)):
        value_layer = lax.index_in_dim(fields, node_layer, 3, False)
        speed_layer = lax.index_in_dim(mesh_speed, node_layer, 3, False)
        slope_layer = lax.index_in_dim(slopes_z, node_layer, 3, False)
        traction = traction_scale * normal * slope_layer[0:3]
        pressure = -normal * value_layer[3]
        mismatch = normal * (value_layer[2] - speed_layer[2])
        both_sides.append(jnp.concatenate([traction, pressure[None], mismatch[None]], 0))
    return jnp.stack(both_sides, 3)

def face_loads(blocks, projection):
    combined = jnp.stack([blocks[0], blocks[1], blocks[2] + blocks[3] + mismatch_gain * blocks[4]])
    return jnp.einsum('ab,cb...->ca...', projection, combined, precision=lax.Precision.HIGHEST)

def place_top(face_force):
    leading = face_force.shape[:-3]
    element_count = face_force.shape[-1]
    upper_layer = face_force.reshape(leading + (3, 3, 3, 1, element_count))
    zeroed = jnp.zeros(leading + (3, 3, 3, 2, element_count), jnp.float32)
    return jnp.concatenate([zeroed, upper_layer], -2).reshape(leading + (81, element_count))

def top_nodes(values):
    leading = values.shape[:-2]
    element_count = values.shape[-1]
    layered = values.reshape(leading + (3, 3, 3, 3, element_count))[..., 2, :]
    return layered.reshape(leading + (3, 9, element_count))

def solid_sweeps(displacement, loads_full, moduli, stiffness):
    diagonal = jnp.diagonal(stiffness)
    divisor = moduli[..., None, :] * diagonal[:, None]
    current = displacement
    for sweep_index in range(SWEEPS):
        product = jnp.einsum('ab,...be->...ae', stiffness, current, precision=lax.Precision.HIGHEST)
        current = current + relaxation * (loads_full - moduli[..., None, :] * product) / divisor
    return current

def blend_faces(face_values):
    upward = (jnp.arange(5, dtype=jnp.float32) / 4.0).reshape(1, 1, 1, 5, 1, 1, 1)
    lower_face = face_values[:, :, :, 0:1]
    upper_face = face_values[:, :, :, 1:2]
    return lower_face * (1.0 - upward) + upper_face * upward

def reference(fluid_state, mesh_velocity, metric, wall_face, wall_owner, wall_target, solid_disp, modulus, stiffness):
    solid_groups = N_GRP // 4
    fluid_groups = N_GRP - solid_groups
    columns = N_GX * N_GY
    elements = BX * BY * BZ
    span_x = BX * N_GX
    span_y = BY * N_GY
    matrix = derivative_table()
    projection, interpolation = face_tables()
    face_ids = wall_face.reshape(N_GRP, N_GX, N_GY, WALL)
    owner_ids = wall_owner.reshape(N_GRP, N_GX, N_GY, WALL)
    target_ids = wall_target.reshape(N_GRP, N_GX, N_GY, WALL)
    index_x = jnp.broadcast_to(jnp.arange(N_GX, dtype=jnp.int32)[:, None, None], (N_GX, N_GY, WALL))
    index_y = jnp.broadcast_to(jnp.arange(N_GY, dtype=jnp.int32)[None, :, None], (N_GX, N_GY, WALL))
    solid_force = jnp.zeros((solid_groups * columns, 3, 9, SE), jnp.float32)
    fluid_next = []
    owners_kept = []
    for group_number in range(fluid_groups):
        walled = jnp.zeros((N_GX, N_GY, 2 * elements), jnp.float32).at[index_x, index_y, face_ids[group_number]].set(1.0)
        walled = walled.reshape(N_GX, N_GY, 2, BX, BY, BZ).transpose(2, 0, 3, 1, 4, 5).reshape(2, span_x, span_y, BZ)
        open_low = 1.0 - walled[0]
        open_high = 1.0 - walled[1]
        start_fields = fluid_state[group_number].astype(jnp.float32).reshape(4, 5, 5, 5, span_x, span_y, BZ)
        mesh_speed = mesh_velocity[group_number].astype(jnp.float32).reshape(3, 5, 5, 5, span_x, span_y, BZ)
        first_changes, unused = rate_terms(start_fields, mesh_speed, metric[group_number], matrix, open_low, open_high)
        middle = start_fields + time_step * first_changes
        second_changes, gradient = rate_terms(middle, mesh_speed, metric[group_number], matrix, open_low, open_high)
        advanced = start_fields + 0.5 * time_step * (first_changes + second_changes)
        fluid_next.append(advanced.reshape(4, 125, span_x, span_y, BZ).astype(jnp.bfloat16))
        blocks = wall_blocks(middle, mesh_speed, gradient[2])
        per_device = blocks.reshape(125, 2, N_GX, BX, N_GY, BY, BZ).transpose(2, 4, 0, 1, 3, 5, 6).reshape(N_GX, N_GY, 125, 2 * elements)
        wall_rows = jnp.take_along_axis(per_device, face_ids[group_number][:, :, None, :], axis=3)
        load_values = face_loads(wall_rows.reshape(N_GX, N_GY, 5, 25, WALL).transpose(2, 3, 0, 1, 4), projection)
        owner_index = group_number % solid_groups * columns + owner_ids[group_number]
        solid_force = solid_force.at[owner_index.reshape(-1), :, :, target_ids[group_number].reshape(-1)].add(load_values.reshape(3, 9, -1).transpose(2, 0, 1))
        owners_kept.append(owner_index)
    solid_start = solid_disp[fluid_groups:].reshape(solid_groups, 81, columns, SE).transpose(0, 2, 1, 3).reshape(solid_groups * columns, 81, SE)
    moduli = modulus[fluid_groups:].reshape(solid_groups * columns, SE)
    solved = solid_sweeps(solid_start, place_top(solid_force), moduli, stiffness)
    nodal_values = jnp.concatenate([top_nodes(solved), top_nodes(solved - solid_start)], 1)
    solid_blocks = solved.reshape(solid_groups, columns, 81, SE).transpose(0, 2, 1, 3).reshape(solid_groups, 81, columns * SE)
    solid_next = jnp.concatenate([jnp.zeros((fluid_groups, 81, columns * SE), jnp.float32), solid_blocks], 0)
    motions = []
    for group_number in range(fluid_groups):
        mesh_speed = mesh_velocity[group_number].astype(jnp.float32).reshape(3, 5, 5, 5, span_x, span_y, BZ)
        picked = nodal_values[owners_kept[group_number], :, :, target_ids[group_number]]
        values = jnp.einsum('pa,...ca->...cp', interpolation, picked, precision=lax.Precision.HIGHEST)
        gathered = jnp.zeros((N_GX, N_GY, 6, 25, 2 * elements), jnp.float32).at[index_x, index_y, :, :, face_ids[group_number]].add(values)
        global_faces = gathered.reshape(N_GX, N_GY, 6, 5, 5, 2, BX, BY, BZ).transpose(2, 3, 4, 5, 0, 6, 1, 7, 8).reshape(6, 5, 5, 2, span_x, span_y, BZ)
        blended = blend_faces(global_faces)
        motion = jnp.concatenate([blended[0:3], mesh_speed + blended[3:6]], 0)
        motions.append(motion.reshape(6, 125, span_x, span_y, BZ).astype(jnp.bfloat16))
    for group_number in range(solid_groups):
        fluid_next.append(jnp.zeros((4, 125, span_x, span_y, BZ), jnp.bfloat16))
        motions.append(jnp.zeros((6, 125, span_x, span_y, BZ), jnp.bfloat16))
    return (jnp.stack(fluid_next), jnp.stack(motions), solid_next)
```

```python
import functools
import math

import jax
import jax.numpy as jnp
import numpy as np
from jax import lax
from jax.experimental import pallas as pl
from jax.experimental.pallas import tpu as pltpu
from jax.sharding import PartitionSpec as P

F32 = jnp.float32
BF16 = jnp.bfloat16
I32 = jnp.int32

FLUID = 6
SOLID = 2
LEVELS = 3
GX = 8
GY = 4
COLS = GX * GY
DT = 0.05
NU = 0.02
RELAX = 0.8


def points_5():
    return np.array([-1.0, -math.sqrt(3.0 / 7.0), 0.0, math.sqrt(3.0 / 7.0), 1.0])


def weights_5():
    return np.array([0.1, 49.0 / 90.0, 32.0 / 45.0, 49.0 / 90.0, 0.1])


def lagrange_table(centres, points):
    result = np.ones((len(points), len(centres)))
    for column in range(len(centres)):
        for partner in range(len(centres)):
            if partner != column:
                result[:, column] *= (points - centres[partner]) / (
                    centres[column] - centres[partner]
                )
    return result


def derivative_table():
    pts = points_5()
    n = len(pts)
    w = np.ones(n)
    for c in range(n):
        for p in range(n):
            if p != c:
                w[c] = w[c] / (pts[c] - pts[p])
    d = np.zeros((n, n))
    for r in range(n):
        for c in range(n):
            if r != c:
                d[r, c] = w[c] / w[r] / (pts[r] - pts[c])
        d[r, r] = -np.sum(d[r])
    return d.astype(np.float32).astype(np.float64)


def split_np(x):
    hi = np.asarray(x, np.float32).astype(jnp.bfloat16)
    lo = (np.asarray(x, np.float64) - hi.astype(np.float64)).astype(np.float32).astype(jnp.bfloat16)
    return hi, lo


def build_tables():
    d = derivative_table()
    eye = np.eye(5)
    first = [
        np.kron(np.kron(d, eye), eye),
        np.kron(np.kron(eye, d), eye),
        np.kron(np.kron(eye, eye), d),
    ]
    volume = np.zeros((768, 128))
    for k in range(3):
        volume[128 * k : 128 * k + 125, :125] = first[k]
        volume[384 + 128 * k : 384 + 128 * k + 125, :125] = first[k] @ first[k]
    face_pick = np.zeros((192, 128))
    face_slope = np.zeros((192, 128))
    node = np.arange(125).reshape(5, 5, 5)
    for k in range(3):
        for side in range(2):
            ids = np.take(node, 4 * side, axis=k).reshape(25)
            rows = 64 * k + 32 * side + np.arange(25)
            face_pick[rows, ids] = 1.0
            face_slope[rows, :125] = first[k][ids]
    values = lagrange_table(np.array([-1.0, 0.0, 1.0]), points_5())
    project_one = (values * weights_5()[:, None]).T
    project = np.kron(project_one, project_one).astype(np.float32).astype(np.float64)
    interp = np.kron(values, values).astype(np.float32).astype(np.float64)
    load = np.zeros((32, 96))
    for c in range(3):
        load[9 * c : 9 * c + 9, 32 * c : 32 * c + 25] = project
    blend = np.zeros((768, 128))
    for ch in range(6):
        for nd in range(125):
            ij, k = nd // 5, nd % 5
            for side, scale in ((0, 1.0 - k / 4.0), (1, k / 4.0)):
                base = 64 * side + 32 * (ch // 3) + 9 * (ch % 3)
                blend[128 * ch + nd, base : base + 9] = scale * interp[ij]
    vol_hi, vol_lo = split_np(volume)
    fs_hi, fs_lo = split_np(face_slope)
    load_hi, load_lo = split_np(load)
    blend_hi, blend_lo = split_np(blend)
    return dict(
        volume=np.concatenate([vol_hi, vol_lo], 1),
        slope=np.concatenate([fs_hi, fs_lo], 1),
        pick=face_pick.astype(jnp.bfloat16),
        inject=np.ascontiguousarray(face_pick.T).astype(jnp.bfloat16),
        load=np.concatenate([load_hi, load_lo], 1),
        blend=np.concatenate([blend_hi, blend_lo], 1),
    )


def mm(a, b):
    return jnp.dot(a, b, preferred_element_type=F32)


def mm_nt(a, b):
    return lax.dot_general(a, b, (((1,), (1,)), ((), ())), preferred_element_type=F32)


def mm_full(a, b):
    return jnp.dot(a, b, preferred_element_type=F32, precision=lax.Precision.HIGHEST)


def split(x):
    hi = x.astype(BF16)
    return hi, (x - hi.astype(F32)).astype(BF16)


def iota(shape, axis):
    return lax.broadcasted_iota(I32, shape, axis)


def as_bf16(mask):
    return jnp.where(mask, 1.0, 0.0).astype(BF16)


def table_times(table, hi, lo=None):
    k = table.shape[1] // 2
    out = mm(table, jnp.concatenate([hi, hi], 0))
    if lo is not None:
        out = out + mm(table[:, :k], lo)
    return out


def unpack_nodes(raw, count):
    parts = []
    r, c = iota((256, 256), 0), iota((256, 256), 1)
    y, n = r >> 7, r & 127
    for f in range(count):
        pick = as_bf16((c == 2 * f + 2 * n + y) & (n < 125))
        window = raw[248 * f : 248 * f + 256, :].astype(BF16)
        both = mm(pick, window).astype(BF16)
        parts += [both[0:128, :], both[128:256, :]]
    return jnp.concatenate(parts, 1)


def metric_row(metric, k):
    row = metric[k : k + 1, :]
    return jnp.concatenate([row] * 4, 1)


def face_values(tables, metric, hi, lo):
    pick, slope = tables
    s = mm(pick, hi)
    if lo is not None:
        s = s + mm(pick, lo)
    g = table_times(slope, hi, lo)
    plus, minus, scaled = [], [], []
    for k in range(3):
        m = metric_row(metric, k)
        rows = slice(64 * k, 64 * k + 64)
        mg = m * g[rows]
        a, b = 0.5 * mg, 2.0 * s[rows]
        plus.append(a + b)
        minus.append(a - b)
        scaled.append(mg)
    return plus, minus, s, scaled


def column_blocks(x, y):
    return jnp.concatenate([x[:, 256 * f + 128 * y : 256 * f + 128 * y + 128] for f in range(4)], 1)


def place_blocks(x, y):
    parts = []
    zero = jnp.zeros((x.shape[0], 128), F32)
    for f in range(4):
        pair = [zero, zero]
        pair[y] = x[:, 128 * f : 128 * f + 128]
        parts += pair
    return jnp.concatenate(parts, 1)


def shift_z(x, step):
    blocks = []
    for b in range(x.shape[1] // 128):
        blocks.append(pltpu.roll(x[:, 128 * b : 128 * b + 128], step % 128, 1))
    return jnp.concatenate(blocks, 1)


def local_faces(plus, minus, open_lo, open_hi):
    lo_x, hi_x = minus[0][0:32], -plus[0][32:64]
    in_lo = place_blocks(column_blocks(minus[1][32:64], 0), 1)
    in_hi = place_blocks(column_blocks(plus[1][0:32], 1), 0)
    lo_y, hi_y = minus[1][0:32] - in_lo, in_hi - plus[1][32:64]
    nb_lo = shift_z(minus[2][32:64], 1) * open_lo
    nb_hi = shift_z(plus[2][0:32], -1) * open_hi
    lo_z, hi_z = minus[2][0:32] - nb_lo, nb_hi - plus[2][32:64]
    return [lo_x, hi_x, lo_y, hi_y, lo_z, hi_z]


def send_faces(plus, minus):
    return (
        plus[0][0:32],
        minus[0][32:64],
        column_blocks(plus[1][0:32], 0),
        column_blocks(minus[1][32:64], 1),
    )


def remote_faces(rx_lo, rx_hi, ry_lo, ry_hi):
    return [-rx_lo, rx_hi, place_blocks(-ry_lo, 0), place_blocks(ry_hi, 1)]


def inject_faces(inject, faces):
    hi, lo = split(jnp.concatenate(faces, 0))
    k = hi.shape[0]
    return mm(inject[:, 0:k], hi) + mm(inject[:, 0:k], lo)


def open_rows(meta):
    return (
        jnp.concatenate([meta[2:3, 0:256]] * 4, 1),
        jnp.concatenate([meta[3:4, 0:256]] * 4, 1),
    )


def volume_rate(volume, metric, fields, hi, lo, wm):
    blocks = []
    carrier = [
        fields[:, 256 * k : 256 * k + 256] - wm[:, 256 * k : 256 * k + 256].astype(F32)
        for k in range(3)
    ]
    m = [metric[k : k + 1, :] for k in range(3)]
    flow = [carrier[k] * m[k] for k in range(3)]
    curve = [NU * m[k] * m[k] for k in range(3)]
    part_lo = None if lo is None else lo[:, 768:1024]
    press = table_times(volume[0:384], hi[:, 768:1024], part_lo)
    div = None
    for c in range(3):
        cols = slice(256 * c, 256 * c + 256)
        part_lo = None if lo is None else lo[:, cols]
        der = table_times(volume, hi[:, cols], part_lo)
        rate = -m[c] * press[128 * c : 128 * c + 128]
        for k in range(3):
            rate = rate + curve[k] * der[384 + 128 * k : 512 + 128 * k]
            rate = rate - flow[k] * der[128 * k : 128 * k + 128]
        own = m[c] * der[128 * c : 128 * c + 128]
        div = own if div is None else div + own
        blocks.append(rate)
    blocks.append(-div)
    return jnp.concatenate(blocks, 1)


def wall_meta(face, owner):
    d = as_bf16(iota((32, 256), 0) == owner)
    before = as_bf16(iota((256, 256), 0) < iota((256, 256), 1))
    count = mm(d, before)
    slot = jnp.sum(jnp.where(iota((32, 256), 0) == owner, count, 0.0), 0, keepdims=True).astype(I32)
    hit = as_bf16(iota((512, 256), 0) == face)
    walled = mm_nt(jnp.ones((8, 256), BF16), hit)[0:1, :]
    z = iota((1, 256), 1) & 127
    open_lo = jnp.where(z == 0, 0.0, 1.0 - walled[:, 0:256])
    open_hi = jnp.where(z == 127, 0.0, 1.0 - walled[:, 256:512])
    row0 = (owner * 4 + (slot >> 2)).astype(F32)
    row1 = (slot & 3).astype(F32)
    return jnp.concatenate([row0, row1, open_lo, open_hi, jnp.zeros((4, 256), F32)], 0)


def slot_matrix(meta):
    return as_bf16(iota((128, 256), 0) == meta[0:1, :].astype(I32))


def quarter_mask(meta):
    return (iota((128, 256), 0) >> 5) == meta[1:2, :].astype(I32)


def to_slots(meta, rows):
    hi, lo = split(jnp.where(quarter_mask(meta), rows, 0.0))
    a = slot_matrix(meta)
    return mm_nt(a, hi) + mm_nt(a, lo)


def from_slots(meta, packed):
    hi, lo = split(packed.T)
    a = slot_matrix(meta)
    wide = jnp.where(quarter_mask(meta), mm(hi, a) + mm(lo, a), 0.0)
    return (wide[0:32] + wide[32:64]) + (wide[64:96] + wide[96:128])


def wall_loads(load, pick, metric, s, scaled_z, wm):
    wz = mm(pick[128:192], wm[:, 512:768])
    out = []
    for side, sign in ((0, -1.0), (1, 1.0)):
        g = scaled_z[32 * side : 32 * side + 32]
        v = s[128 + 32 * side : 160 + 32 * side]
        parts = [0.2 * sign * g[:, 0:256], 0.2 * sign * g[:, 256:512]]
        w = wz[32 * side : 32 * side + 32]
        parts.append(
            sign * (0.2 * g[:, 512:768] - v[:, 768:1024] + 0.5 * (v[:, 512:768] - w))
        )
        hi, lo = split(jnp.concatenate(parts, 0))
        out.append(table_times(load, hi, lo))
    return jnp.concatenate(out, 1)


def is_fluid():
    return lax.axis_index("grp") < FLUID


def kernel_1(
    state, speed, metric, face, owner, target, stiff, volume, slope, pick, inject,
    u0_o, wm_o, part_o, meta_o, sxl_o, sxh_o, syl_o, syh_o, tgt_o, pow_o, load_o, top_o,
):
    @pl.when(is_fluid())
    def _():
        u0 = unpack_nodes(state[...].astype(F32), 4)
        wm = unpack_nodes(speed[...].astype(F32), 3)
        u0_o[...] = u0
        wm_o[...] = wm
        meta = wall_meta(face[...], owner[...])
        meta_o[...] = meta
        met = metric[...]
        plus, minus, _, _ = face_values((pick[...], slope[...]), met, u0, None)
        sxl, sxh, syl, syh = send_faces(plus, minus)
        sxl_o[...] = sxl
        sxh_o[...] = sxh
        syl_o[...] = syl
        syh_o[...] = syh
        rate = volume_rate(volume[...], met, u0.astype(F32), u0, None, wm)
        faces = local_faces(plus, minus, *open_rows(meta))
        part_o[...] = rate + inject_faces(inject[...], faces)
        rows = jnp.broadcast_to((target[...] + 1).astype(F32), (128, 256))
        tgt_o[...] = to_slots(meta, rows)

    @pl.when(jnp.logical_not(is_fluid()))
    def _():
        pow_, load, top = solid_tables(stiff[...])
        pow_o[...] = pow_
        load_o[...] = load
        top_o[...] = top


def solid_tables(k):
    r, c = iota((128, 128), 0), iota((128, 128), 1)
    eye = r == c
    diag = jnp.where(eye, k, 0.0)
    col = jnp.sum(diag, 1, keepdims=True)
    row = jnp.sum(diag, 0, keepdims=True)
    one = jnp.where(eye, 1.0, 0.0)
    s = one - RELAX * k / col
    s2 = mm_full(s, s)
    s4 = mm_full(s2, s2)
    t = mm_full(one + s, one + s2) * (RELAX / row)
    sel = jnp.where((c == 3 * (r & 31) + 2) & ((r & 31) < 27), 1.0, 0.0)
    load = mm_full(t, sel.T)
    top = mm_full(sel, load).T
    return s4, load, top


def kernel_2(
    part, rxl, rxh, ryl, ryh, metric, u0, wm, meta_r, face, slope, pick, inject, load,
    disp_any, modulus, pow_, tgt,
    v1_o, sxl_o, sxh_o, syl_o, syh_o, pay_o, base_o, d0_o, inv_o,
    disp, wide, sem,
):
    @pl.when(is_fluid())
    def _():
        gx, gy = lax.axis_index("gx"), lax.axis_index("gy")
        meta = meta_r[...]
        met = metric[...]
        zero = jnp.zeros((), F32)
        faces = remote_faces(
            jnp.where(gx > 0, rxl[...], zero),
            jnp.where(gx < GX - 1, rxh[...], zero),
            jnp.where(gy > 0, ryl[...], zero),
            jnp.where(gy < GY - 1, ryh[...], zero),
        )
        rate = part[...] + inject_faces(inject[...], faces)
        v1 = u0[...].astype(F32) + DT * rate
        v1_o[...] = v1
        hi, lo = split(v1)
        plus, minus, s, scaled = face_values((pick[...], slope[...]), met, hi, lo)
        sxl, sxh, syl, syh = send_faces(plus, minus)
        sxl_o[...] = sxl
        sxh_o[...] = sxh
        syl_o[...] = syl
        syh_o[...] = syh
        loads = wall_loads(load[...], pick[...], met, s, scaled[2], wm[...])
        lh, ll = split(loads)
        hit = as_bf16(iota((512, 256), 0) == face[...])
        rows = mm(lh, hit) + mm(ll, hit)
        pay_o[...] = to_slots(meta, jnp.concatenate([rows] * 4, 0))

    @pl.when(jnp.logical_not(is_fluid()))
    def _():
        copy = pltpu.make_async_copy(disp_any, disp, sem)
        copy.start()
        copy.wait()
        d = disp[...]
        r, c = iota((32, 81), 0), iota((32, 81), 1)
        sel = as_bf16((c == 3 * r + 2) & (r < 27))
        r, c = iota((32, 128), 0), iota((32, 128), 1)
        sel_wide = jnp.where((c == 3 * r + 2) & (r < 27), 1.0, 0.0)
        ph, plo = split(mm_full(sel_wide, pow_[...])[:, 0:81])
        dh, dl = split(d)
        base = mm(ph, dh) + (mm(ph, dl) + mm(plo, dh))
        inv = jnp.broadcast_to(1.0 / modulus[...], (32, 4096))
        base = jnp.where(iota((32, 4096), 0) == 27, inv, base)
        bh, bl = split(base)
        wide[0:32, :] = bh
        wide[32:64, :] = bl
        wide[64:96, :] = mm(sel, dh).astype(BF16)
        wide[96:128, :] = mm(sel, dl).astype(BF16)
        targets = tgt[...].astype(I32) - 1
        lane = iota((384, 128), 1)
        base_a = jnp.zeros((384, 128), F32)
        d0_a = jnp.zeros((384, 128), F32)
        inv_a = jnp.zeros((384, 128), F32)
        for q in range(4):
            column = targets[:, 32 * q : 32 * q + 1]
            got = jnp.zeros((384, 128), F32)
            for part_e in range(4):
                e = iota((384, 1024), 1) + 1024 * part_e
                one = as_bf16(e == column)
                got = got + mm_nt(one, wide[:, 1024 * part_e : 1024 * part_e + 1024])
            both = got + pltpu.roll(got, 96, 1)
            here = (lane >> 5) == q
            shift = 32 * q
            base_q = pltpu.roll(both, shift, 1) if shift else both
            d0_q = pltpu.roll(both, (shift + 64) % 128, 1)
            inv_q = jnp.broadcast_to(both[:, 27:28], (384, 128))
            base_a = jnp.where(here, base_q, base_a)
            d0_a = jnp.where(here, d0_q, d0_a)
            inv_a = jnp.where(here, inv_q, inv_a)
        base_o[...] = base_a
        d0_o[...] = d0_a
        inv_o[...] = inv_a


def kernel_3(
    v1, rxl, rxh, ryl, ryh, metric, u0, wm, meta_r, volume, slope, pick, inject,
    pay, tgt, base, inv, top,
    next_o, row_o,
    stage, gathered,
):
    @pl.when(is_fluid())
    def _():
        gx, gy = lax.axis_index("gx"), lax.axis_index("gy")
        met = metric[...]
        zero = jnp.zeros((), F32)
        fields = v1[...]
        hi, lo = split(fields)
        plus, minus, _, _ = face_values((pick[...], slope[...]), met, hi, lo)
        faces = local_faces(plus, minus, *open_rows(meta_r[...]))
        far = remote_faces(
            jnp.where(gx > 0, rxl[...], zero),
            jnp.where(gx < GX - 1, rxh[...], zero),
            jnp.where(gy > 0, ryl[...], zero),
            jnp.where(gy < GY - 1, ryh[...], zero),
        )
        faces = [a + b for a, b in zip(faces[:4], far)] + faces[4:]
        rate = volume_rate(volume[...], met, fields, hi, lo, wm[...])
        rate = rate + inject_faces(inject[...], faces)
        result = 0.5 * (u0[...].astype(F32) + fields) + (0.5 * DT) * rate
        result = result.astype(BF16)
        stage[...] = jnp.zeros((1000, 128), F32)
        r, c = iota((256, 256), 0), iota((256, 256), 1)
        for f in range(4):
            local_r = r - 2 * f
            put = as_bf16((local_r >= 0) & (local_r < 250) & (c == (local_r >> 1) + 128 * (local_r & 1)))
            block = result[:, 256 * f : 256 * f + 256]
            pair = jnp.concatenate([block[:, 0:128], block[:, 128:256]], 0)
            stage[248 * f : 248 * f + 256, :] = stage[248 * f : 248 * f + 256, :] + mm(put, pair)
        next_o[...] = stage[...].astype(BF16)

    @pl.when(jnp.logical_not(is_fluid()))
    def _():
        next_o[...] = jnp.zeros((1000, 128), BF16)
        loads = pay[...]
        targets = tgt[...]
        turned = targets.T
        lane = iota((384, 128), 1)
        for q in range(4):
            h, l = split(jnp.where((lane >> 5) == q, loads, 0.0))
            gathered[384 * q : 384 * q + 384, 0:128] = h
            gathered[384 * q : 384 * q + 384, 128:256] = l
        row = jnp.concatenate([turned[32 * q : 32 * q + 1, :] for q in range(4)], 1)
        th, tl = split(top[...])
        total = jnp.zeros((384, 128), F32)
        for q in range(4):
            same = as_bf16(targets[:, 32 * q : 32 * q + 1] == row)
            acc = mm(same, gathered[...])
            ah, al = split(acc[:, 0:128] + acc[:, 128:256])
            res = mm(ah, th) + (mm(al, th) + mm(ah, tl))
            total = jnp.where((lane >> 5) == q, res, total)
        row_o[...] = base[...] + inv[...] * total


def kernel_4(
    dn, d0, meta_r, face, wm, blend,
    disp_any, modulus, pow_, load, pay, tgt,
    motion_o, solid_any,
    disp, out, gathered, sem, sem_o,
):
    @pl.when(is_fluid())
    def _():
        out[...] = jnp.zeros((81, 4096), F32)
        copy = pltpu.make_async_copy(out, solid_any, sem_o)
        copy.start()
        meta = meta_r[...]
        a = from_slots(meta, dn[...])
        b = from_slots(meta, d0[...])
        rows = jnp.concatenate([a, a - b], 0)
        hi, lo = split(rows)
        hit = as_bf16(iota((512, 256), 0) == face[...])
        faces = mm_nt(hi, hit) + mm_nt(lo, hit)
        faces = jnp.concatenate([faces[:, 0:256], faces[:, 256:512]], 0)
        hi, lo = split(faces)
        for ch in range(6):
            value = table_times(blend[128 * ch : 128 * ch + 128, :], hi, lo)
            if ch >= 3:
                value = value + wm[:, 256 * (ch - 3) : 256 * (ch - 3) + 256].astype(F32)
            motion_o[:, 256 * ch : 256 * ch + 256] = value.astype(BF16)
        copy.wait()

    @pl.when(jnp.logical_not(is_fluid()))
    def _():
        copy = pltpu.make_async_copy(disp_any, disp, sem)
        copy.start()
        motion_o[...] = jnp.zeros((128, 1536), BF16)
        loads = pay[...]
        turned = tgt[...].T.astype(I32) - 1
        lane = iota((384, 128), 1)
        for q in range(4):
            part = pltpu.roll(loads, (128 - 32 * q) % 128, 1) if q else loads
            part = jnp.where(lane < 32, part, 0.0)
            h, l = split(part)
            gathered[384 * q : 384 * q + 384, :] = jnp.where(
                lane < 32, h.astype(F32), pltpu.roll(l.astype(F32), 32, 1)
            ).astype(BF16)
        th, tl = split(load[...][0:81, :])
        sh, sl = split(pow_[...][0:81, 0:81])
        rows = jnp.concatenate([turned[32 * q : 32 * q + 1, :] for q in range(4)], 1)
        copy.wait()
        fold_r, fold_c = iota((128, 128), 0), iota((128, 128), 1)
        fold = as_bf16((fold_r == (fold_c & 31)) & (fold_c < 64))
        table = (mm(th, fold), mm(tl, fold))
        table = (table[0].astype(BF16), table[1].astype(BF16))
        for part_e in range(16):
            cols = slice(256 * part_e, 256 * part_e + 256)
            one = as_bf16(iota((256, 1536), 0) + 256 * part_e == rows)
            force = mm(one, gathered[...])
            fh, fl = split(force)
            add = mm_nt(table[0], fh) + (mm_nt(table[0], fl) + mm_nt(table[1], fh))
            d = disp[:, cols]
            dh, dl = split(d)
            keep = mm(sh, dh) + (mm(sh, dl) + mm(sl, dh))
            out[:, cols] = keep + add / modulus[:, cols]
        copy = pltpu.make_async_copy(out, solid_any, sem_o)
        copy.start()
        copy.wait()


MESH = pl.DeviceIdType.MESH


def at(grp, gx, gy):
    return dict(device_id=(grp, gx, gy), device_id_type=MESH)


def transfer(
    faces_in, pay_in, faces_out, pay_out, send, recv, psend, precv
):
    grp, gx, gy = lax.axis_index("grp"), lax.axis_index("gx"), lax.axis_index("gy")
    fluid = grp < FLUID
    solid = jnp.logical_not(fluid)
    barrier = pltpu.get_barrier_semaphore()
    column = gx * GY + gy
    has = [gx > 0, gx < GX - 1, gy > 0, gy < GY - 1]
    where = [(grp, gx - 1, gy), (grp, gx + 1, gy), (grp, gx, gy - 1), (grp, gx, gy + 1)]
    owner_group = FLUID + lax.rem(grp, SOLID)

    for k in range(4):
        @pl.when(fluid & has[k])
        def _():
            pl.semaphore_signal(barrier, inc=1, **at(*where[k]))

    @pl.when(solid)
    def _():
        def greet(i, carry):
            g = lax.rem(i, LEVELS) * SOLID + (grp - FLUID)
            c = lax.rem(i // LEVELS + column, COLS)
            pl.semaphore_signal(barrier, inc=1, **at(g, c // GY, lax.rem(c, GY)))
            return carry
        lax.fori_loop(0, LEVELS * COLS, greet, 0)

    @pl.when(fluid)
    def _():
        peers = jnp.int32(COLS)
        for k in range(4):
            peers = peers + jnp.where(has[k], 1, 0)
        pl.semaphore_wait(barrier, peers)

    other = [1, 0, 3, 2]
    copies = []
    for k in range(4):
        copy = pltpu.make_async_remote_copy(
            faces_in[k], faces_out[other[k]], send.at[k], recv.at[other[k]], **at(*where[k])
        )
        copies.append(copy)

        @pl.when(fluid & has[k])
        def _():
            copy.start()

    @pl.when(fluid)
    def _():
        row = (grp // SOLID) * COLS + column

        def push(i, carry):
            o = lax.rem(i + column, COLS)
            pltpu.make_async_remote_copy(
                pay_in.at[o], pay_out.at[row], psend, precv,
                **at(owner_group, o // GY, lax.rem(o, GY)),
            ).start()
            return carry
        lax.fori_loop(0, COLS, push, 0)

    for k in range(4):
        @pl.when(fluid & has[k])
        def _():
            copies[k].wait_send()
            pltpu.make_async_remote_copy(
                faces_in[k], faces_out[k], send.at[k], recv.at[k], **at(*where[k])
            ).wait_recv()

    @pl.when(fluid)
    def _():
        pltpu.make_async_remote_copy(
            pay_in, pay_out.at[pl.ds(0, COLS)], psend, precv, **at(owner_group, gx, gy)
        ).wait_send()

    @pl.when(solid)
    def _():
        pltpu.make_async_remote_copy(
            pay_out, pay_out, psend, precv, **at(0, gx, gy)
        ).wait_recv()


def send_kernel(sxl, sxh, syl, syh, pay, rxl, rxh, ryl, ryh, got, send, recv, psend, precv):
    transfer((sxl, sxh, syl, syh), pay, (rxl, rxh, ryl, ryh), got, send, recv, psend, precv)


def return_kernel(rows, d0, rows_out, d0_out, psend, precv):
    grp, gx, gy = lax.axis_index("grp"), lax.axis_index("gx"), lax.axis_index("gy")
    fluid = grp < FLUID
    solid = jnp.logical_not(fluid)
    barrier = pltpu.get_barrier_semaphore()
    column = gx * GY + gy
    owner_group = FLUID + lax.rem(grp, SOLID)

    @pl.when(fluid)
    def _():
        def greet(i, carry):
            o = lax.rem(i + column, COLS)
            pl.semaphore_signal(barrier, inc=1, **at(owner_group, o // GY, lax.rem(o, GY)))
            return carry
        lax.fori_loop(0, COLS, greet, 0)

    @pl.when(solid)
    def _():
        pl.semaphore_wait(barrier, LEVELS * COLS)

        def push(i, carry):
            level = lax.rem(i, LEVELS)
            g = level * SOLID + (grp - FLUID)
            c = lax.rem(i // LEVELS + column, COLS)
            to = at(g, c // GY, lax.rem(c, GY))
            src = level * COLS + c
            pltpu.make_async_remote_copy(
                rows.at[src], rows_out.at[column], psend.at[0], precv.at[0], **to
            ).start()
            pltpu.make_async_remote_copy(
                d0.at[src], d0_out.at[column], psend.at[1], precv.at[1], **to
            ).start()
            return carry
        lax.fori_loop(0, LEVELS * COLS, push, 0)
        for k, ref in ((0, rows), (1, d0)):
            pltpu.make_async_remote_copy(
                ref, ref, psend.at[k], precv.at[k], **at(0, gx, gy)
            ).wait_send()

    @pl.when(fluid)
    def _():
        for k, ref in ((0, rows_out), (1, d0_out)):
            pltpu.make_async_remote_copy(
                ref, ref, psend.at[k], precv.at[k], **at(owner_group, gx, gy)
            ).wait_recv()


VM = pl.BlockSpec(memory_space=pltpu.VMEM)
ANY = pl.BlockSpec(memory_space=pl.ANY)


def shape(dims, dtype=F32):
    return jax.ShapeDtypeStruct(dims, dtype)


FACE_SHAPES = [shape((32, 1024)), shape((32, 1024)), shape((32, 512)), shape((32, 512))]


def local(
    fluid_state, mesh_velocity, metric, wall_face, wall_owner, wall_target, solid_disp, modulus,
    stiffness,
):
    tab = {k: jnp.asarray(v) for k, v in build_tables().items()}
    state = fluid_state.reshape(1000, 128)
    speed = jnp.pad(mesh_velocity.reshape(750, 128), ((0, 2), (0, 0)))
    met = metric.reshape(3, 256)
    face = wall_face.reshape(1, 256)
    owner = wall_owner.reshape(1, 256)
    target = wall_target.reshape(1, 256)
    disp = solid_disp.reshape(81, 4096)
    mod = modulus.reshape(1, 4096)
    stiff = jnp.pad(stiffness, ((0, 47), (0, 47))) + jnp.asarray(
        np.diag((np.arange(128) >= 81).astype(np.float32))
    )
    params = pltpu.CompilerParams(vmem_limit_bytes=60 * 1024 * 1024)

    u0, wm, part, meta, sxl, sxh, syl, syh, tgt, pow_, load, top = pl.pallas_call(
        kernel_1,
        out_shape=[
            shape((128, 1024), BF16), shape((128, 768), BF16), shape((128, 1024)), shape((8, 256)),
            *FACE_SHAPES, shape((128, 128)), shape((128, 128)), shape((128, 128)),
            shape((128, 128)),
        ],
        in_specs=[VM] * 11,
        out_specs=[VM] * 12,
        compiler_params=params,
        name="fluid_first",
    )(state, speed, met, face, owner, target, stiff, tab["volume"], tab["slope"], tab["pick"],
      tab["inject"])

    def send(cid, faces, pay, name):
        return pl.pallas_call(
            send_kernel,
            out_shape=[*FACE_SHAPES, shape((LEVELS * COLS, 4, 128))],
            in_specs=[ANY] * 5,
            out_specs=[ANY] * 5,
            scratch_shapes=[
                pltpu.SemaphoreType.DMA((4,)), pltpu.SemaphoreType.DMA((4,)),
                pltpu.SemaphoreType.DMA, pltpu.SemaphoreType.DMA,
            ],
            compiler_params=pltpu.CompilerParams(collective_id=cid, has_side_effects=True),
            name=name,
        )(*faces, pay.reshape(COLS, 4, 128))

    rxl, rxh, ryl, ryh, got_t = send(0, (sxl, sxh, syl, syh), tgt, "send_first")
    got_t = got_t.reshape(384, 128)

    v1, sxl, sxh, syl, syh, pay, base, d0, inv = pl.pallas_call(
        kernel_2,
        out_shape=[
            shape((128, 1024)), *FACE_SHAPES, shape((128, 128)), shape((384, 128)),
            shape((384, 128)), shape((384, 128)),
        ],
        in_specs=[VM] * 14 + [ANY] + [VM] * 3,
        out_specs=[VM] * 9,
        scratch_shapes=[
            pltpu.VMEM((81, 4096), F32), pltpu.VMEM((128, 4096), BF16), pltpu.SemaphoreType.DMA,
        ],
        compiler_params=params,
        name="fluid_middle",
    )(part, rxl, rxh, ryl, ryh, met, u0, wm, meta, face, tab["slope"], tab["pick"],
      tab["inject"], tab["load"], disp, mod, pow_, got_t)

    rxl, rxh, ryl, ryh, got_p = send(1, (sxl, sxh, syl, syh), pay, "send_second")
    got_p = got_p.reshape(384, 128)

    fluid_next, rows = pl.pallas_call(
        kernel_3,
        out_shape=[shape((1000, 128), BF16), shape((384, 128))],
        in_specs=[VM] * 18,
        out_specs=[VM] * 2,
        scratch_shapes=[pltpu.VMEM((1000, 128), F32), pltpu.VMEM((1536, 256), BF16)],
        compiler_params=params,
        name="fluid_last",
    )(v1, rxl, rxh, ryl, ryh, met, u0, wm, meta, tab["volume"], tab["slope"], tab["pick"],
      tab["inject"], got_p, got_t, base, inv, top)

    back, back0 = pl.pallas_call(
        return_kernel,
        out_shape=[shape((COLS, 4, 128))] * 2,
        in_specs=[ANY] * 2,
        out_specs=[ANY] * 2,
        scratch_shapes=[pltpu.SemaphoreType.DMA((2,)), pltpu.SemaphoreType.DMA((2,))],
        compiler_params=pltpu.CompilerParams(collective_id=2, has_side_effects=True),
        name="send_back",
    )(rows.reshape(LEVELS * COLS, 4, 128), d0.reshape(LEVELS * COLS, 4, 128))

    motion, solid_next = pl.pallas_call(
        kernel_4,
        out_shape=[shape((128, 1536), BF16), shape((81, 4096))],
        in_specs=[VM] * 6 + [ANY] + [VM] * 5,
        out_specs=[VM, ANY],
        scratch_shapes=[
            pltpu.VMEM((81, 4096), F32), pltpu.VMEM((81, 4096), F32), pltpu.VMEM((1536, 128), BF16),
            pltpu.SemaphoreType.DMA, pltpu.SemaphoreType.DMA,
        ],
        compiler_params=params,
        name="final",
    )(back.reshape(128, 128), back0.reshape(128, 128), meta, face, wm, tab["blend"],
      disp, mod, pow_, load, got_p, got_t)

    motion = motion[0:125].reshape(125, 6, 2, 128).transpose(1, 0, 2, 3)
    return (
        fluid_next.reshape(1, 4, 125, 1, 2, 128),
        motion.reshape(1, 6, 125, 1, 2, 128),
        solid_next.reshape(1, 81, 4096),
    )


def solution(mesh):
    in_specs = (
        P("grp", None, None, "gx", "gy", None),
        P("grp", None, None, "gx", "gy", None),
        P("grp", None, "gx", "gy", None),
        P(("grp", "gx", "gy")),
        P(("grp", "gx", "gy"), None),
        P(("grp", "gx", "gy")),
        P("grp", None, ("gx", "gy")),
        P("grp", ("gx", "gy")),
        P(),
    )
    out_specs = (
        P("grp", None, None, "gx", "gy", None),
        P("grp", None, None, "gx", "gy", None),
        P("grp", None, ("gx", "gy")),
    )
    return jax.shard_map(local, mesh=mesh, in_specs=in_specs, out_specs=out_specs, check_vma=False)
```

```python
import functools
import math

import jax
import jax.numpy as jnp
import numpy as np
from jax import lax
from jax.experimental import pallas as pl
from jax.experimental.pallas import tpu as pltpu
from jax.sharding import PartitionSpec as P

F32 = jnp.float32
BF16 = jnp.bfloat16
I32 = jnp.int32

FLUID = 6
SOLID = 2
LEVELS = 3
GX = 8
GY = 4
COLS = GX * GY
DT = 0.05
NU = 0.02
RELAX = 0.8


def points_5():
    return np.array([-1.0, -math.sqrt(3.0 / 7.0), 0.0, math.sqrt(3.0 / 7.0), 1.0])


def weights_5():
    return np.array([0.1, 49.0 / 90.0, 32.0 / 45.0, 49.0 / 90.0, 0.1])


def lagrange_table(centres, points):
    result = np.ones((len(points), len(centres)))
    for column in range(len(centres)):
        for partner in range(len(centres)):
            if partner != column:
                result[:, column] *= (points - centres[partner]) / (
                    centres[column] - centres[partner]
                )
    return result


def derivative_table():
    pts = points_5()
    n = len(pts)
    w = np.ones(n)
    for c in range(n):
        for p in range(n):
            if p != c:
                w[c] = w[c] / (pts[c] - pts[p])
    d = np.zeros((n, n))
    for r in range(n):
        for c in range(n):
            if r != c:
                d[r, c] = w[c] / w[r] / (pts[r] - pts[c])
        d[r, r] = -np.sum(d[r])
    return d.astype(np.float32).astype(np.float64)


def split_np(x):
    hi = np.asarray(x, np.float32).astype(jnp.bfloat16)
    lo = (np.asarray(x, np.float64) - hi.astype(np.float64)).astype(np.float32).astype(jnp.bfloat16)
    return hi, lo


def build_tables():
    d = derivative_table()
    eye = np.eye(5)
    first = [
        np.kron(np.kron(d, eye), eye),
        np.kron(np.kron(eye, d), eye),
        np.kron(np.kron(eye, eye), d),
    ]
    volume = np.zeros((768, 128))
    for k in range(3):
        volume[128 * k : 128 * k + 125, :125] = first[k]
        volume[384 + 128 * k : 384 + 128 * k + 125, :125] = first[k] @ first[k]
    face_pick = np.zeros((192, 128))
    face_slope = np.zeros((192, 128))
    node = np.arange(125).reshape(5, 5, 5)
    for k in range(3):
        for side in range(2):
            ids = np.take(node, 4 * side, axis=k).reshape(25)
            rows = 64 * k + 32 * side + np.arange(25)
            face_pick[rows, ids] = 1.0
            face_slope[rows, :125] = first[k][ids]
    values = lagrange_table(np.array([-1.0, 0.0, 1.0]), points_5())
    project_one = (values * weights_5()[:, None]).T
    project = np.kron(project_one, project_one).astype(np.float32).astype(np.float64)
    interp = np.kron(values, values).astype(np.float32).astype(np.float64)
    load = np.zeros((32, 96))
    for c in range(3):
        load[9 * c : 9 * c + 9, 32 * c : 32 * c + 25] = project
    blend = np.zeros((768, 128))
    for ch in range(6):
        for nd in range(125):
            ij, k = nd // 5, nd % 5
            for side, scale in ((0, 1.0 - k / 4.0), (1, k / 4.0)):
                base = 64 * side + 32 * (ch // 3) + 9 * (ch % 3)
                blend[128 * ch + nd, base : base + 9] = scale * interp[ij]
    vol_hi, vol_lo = split_np(volume)
    fs_hi, fs_lo = split_np(face_slope)
    load_hi, load_lo = split_np(load)
    blend_hi, blend_lo = split_np(blend)
    return dict(
        volume=np.concatenate([vol_hi, vol_lo], 1),
        slope=np.concatenate([fs_hi, fs_lo], 1),
        pick=face_pick.astype(jnp.bfloat16),
        inject=np.ascontiguousarray(face_pick.T).astype(jnp.bfloat16),
        load=np.concatenate([load_hi, load_lo], 1),
        blend=np.concatenate([blend_hi, blend_lo], 1),
    )


def mm(a, b):
    return jnp.dot(a, b, preferred_element_type=F32)


def mm_nt(a, b):
    return lax.dot_general(a, b, (((1,), (1,)), ((), ())), preferred_element_type=F32)


def mm_full(a, b):
    return jnp.dot(a, b, preferred_element_type=F32, precision=lax.Precision.HIGHEST)


def split(x):
    hi = x.astype(BF16)
    return hi, (x - hi.astype(F32)).astype(BF16)


def iota(shape, axis):
    return lax.broadcasted_iota(I32, shape, axis)


def as_bf16(mask):
    return jnp.where(mask, 1.0, 0.0).astype(BF16)


def table_times(table, hi, lo=None):
    k = table.shape[1] // 2
    out = mm(table, jnp.concatenate([hi, hi], 0))
    if lo is not None:
        out = out + mm(table[:, :k], lo)
    return out


def unpack_nodes(raw, count, stride):
    parts = []
    r, c = iota((256, 256), 0), iota((256, 256), 1)
    y, n = r >> 7, r & 127
    for f in range(count):
        start = stride * f // 8 * 8
        pick = as_bf16((c == stride * f - start + 2 * n + y) & (n < 125))
        window = raw[start : start + 256, :].astype(BF16)
        both = mm(pick, window).astype(BF16)
        parts += [both[0:128, :], both[128:256, :]]
    return jnp.concatenate(parts, 1)


def metric_row(metric, k):
    row = metric[k : k + 1, :]
    return jnp.concatenate([row] * 4, 1)


def face_values(tables, metric, hi, lo):
    pick, slope = tables
    s = mm(pick, hi)
    if lo is not None:
        s = s + mm(pick, lo)
    g = table_times(slope, hi, lo)
    plus, minus, scaled = [], [], []
    for k in range(3):
        m = metric_row(metric, k)
        rows = slice(64 * k, 64 * k + 64)
        mg = m * g[rows]
        a, b = 0.5 * mg, 2.0 * s[rows]
        plus.append(a + b)
        minus.append(a - b)
        scaled.append(mg)
    return plus, minus, s, scaled


def column_blocks(x, y):
    return jnp.concatenate([x[:, 256 * f + 128 * y : 256 * f + 128 * y + 128] for f in range(4)], 1)


def place_blocks(x, y):
    parts = []
    zero = jnp.zeros((x.shape[0], 128), F32)
    for f in range(4):
        pair = [zero, zero]
        pair[y] = x[:, 128 * f : 128 * f + 128]
        parts += pair
    return jnp.concatenate(parts, 1)


def shift_z(x, step):
    blocks = []
    for b in range(x.shape[1] // 128):
        blocks.append(pltpu.roll(x[:, 128 * b : 128 * b + 128], step % 128, 1))
    return jnp.concatenate(blocks, 1)


def local_faces(plus, minus, open_lo, open_hi):
    lo_x, hi_x = minus[0][0:32], -plus[0][32:64]
    in_lo = place_blocks(column_blocks(minus[1][32:64], 0), 1)
    in_hi = place_blocks(column_blocks(plus[1][0:32], 1), 0)
    lo_y, hi_y = minus[1][0:32] - in_lo, in_hi - plus[1][32:64]
    nb_lo = shift_z(minus[2][32:64], 1) * open_lo
    nb_hi = shift_z(plus[2][0:32], -1) * open_hi
    lo_z, hi_z = minus[2][0:32] - nb_lo, nb_hi - plus[2][32:64]
    return [lo_x, hi_x, lo_y, hi_y, lo_z, hi_z]


def send_faces(plus, minus):
    return (
        plus[0][0:32],
        minus[0][32:64],
        column_blocks(plus[1][0:32], 0),
        column_blocks(minus[1][32:64], 1),
    )


def remote_faces(rx_lo, rx_hi, ry_lo, ry_hi):
    return [-rx_lo, rx_hi, place_blocks(-ry_lo, 0), place_blocks(ry_hi, 1)]


def inject_faces(inject, faces):
    hi, lo = split(jnp.concatenate(faces, 0))
    k = hi.shape[0]
    return mm(inject[:, 0:k], hi) + mm(inject[:, 0:k], lo)


def flat_metric(metric):
    return jnp.concatenate([metric[:, 0, :], metric[:, 1, :]], 1)


def open_rows(meta):
    return (
        jnp.concatenate([meta[2:3, 0:256]] * 4, 1),
        jnp.concatenate([meta[3:4, 0:256]] * 4, 1),
    )


def volume_rate(volume, metric, fields, hi, lo, wm):
    blocks = []
    carrier = [
        fields[:, 256 * k : 256 * k + 256] - wm[:, 256 * k : 256 * k + 256].astype(F32)
        for k in range(3)
    ]
    m = [metric[k : k + 1, :] for k in range(3)]
    flow = [carrier[k] * m[k] for k in range(3)]
    curve = [NU * m[k] * m[k] for k in range(3)]
    part_lo = None if lo is None else lo[:, 768:1024]
    press = table_times(volume[0:384], hi[:, 768:1024], part_lo)
    div = None
    for c in range(3):
        cols = slice(256 * c, 256 * c + 256)
        part_lo = None if lo is None else lo[:, cols]
        der = table_times(volume, hi[:, cols], part_lo)
        rate = -m[c] * press[128 * c : 128 * c + 128]
        for k in range(3):
            rate = rate + curve[k] * der[384 + 128 * k : 512 + 128 * k]
            rate = rate - flow[k] * der[128 * k : 128 * k + 128]
        own = m[c] * der[128 * c : 128 * c + 128]
        div = own if div is None else div + own
        blocks.append(rate)
    blocks.append(-div)
    return jnp.concatenate(blocks, 1)


def wall_meta(face, owner):
    d = as_bf16(iota((32, 256), 0) == owner)
    before = as_bf16(iota((256, 256), 0) < iota((256, 256), 1))
    count = mm(d, before)
    slot = jnp.sum(jnp.where(iota((32, 256), 0) == owner, count, 0.0), 0, keepdims=True).astype(I32)
    hit = as_bf16(iota((512, 256), 0) == face)
    walled = mm_nt(jnp.ones((8, 256), BF16), hit)[0:1, :]
    z = iota((1, 256), 1) & 127
    open_lo = jnp.where(z == 0, 0.0, 1.0 - walled[:, 0:256])
    open_hi = jnp.where(z == 127, 0.0, 1.0 - walled[:, 256:512])
    row0 = (owner * 4 + (slot >> 2)).astype(F32)
    row1 = (slot & 3).astype(F32)
    return jnp.concatenate([row0, row1, open_lo, open_hi, jnp.zeros((4, 256), F32)], 0)


def slot_matrix(meta):
    return as_bf16(iota((128, 256), 0) == meta[0:1, :].astype(I32))


def quarter_mask(meta):
    return (iota((128, 256), 0) >> 5) == meta[1:2, :].astype(I32)


def to_slots(meta, rows):
    hi, lo = split(jnp.where(quarter_mask(meta), rows, 0.0))
    a = slot_matrix(meta)
    return mm_nt(a, hi) + mm_nt(a, lo)


def from_slots(meta, packed):
    hi, lo = split(packed.T)
    a = slot_matrix(meta)
    wide = jnp.where(quarter_mask(meta), mm(hi, a) + mm(lo, a), 0.0)
    return (wide[0:32] + wide[32:64]) + (wide[64:96] + wide[96:128])


def wall_loads(load, pick, metric, s, scaled_z, wm):
    wz = mm(pick[128:192], wm[:, 512:768])
    out = []
    for side, sign in ((0, -1.0), (1, 1.0)):
        g = scaled_z[32 * side : 32 * side + 32]
        v = s[128 + 32 * side : 160 + 32 * side]
        parts = [0.2 * sign * g[:, 0:256], 0.2 * sign * g[:, 256:512]]
        w = wz[32 * side : 32 * side + 32]
        parts.append(
            sign * (0.2 * g[:, 512:768] - v[:, 768:1024] + 0.5 * (v[:, 512:768] - w))
        )
        hi, lo = split(jnp.concatenate(parts, 0))
        out.append(table_times(load, hi, lo))
    return jnp.concatenate(out, 1)


MESH = pl.DeviceIdType.MESH


def is_fluid():
    return lax.axis_index("grp") < FLUID


def at(grp, gx, gy):
    return dict(device_id=(grp, gx, gy), device_id_type=MESH)


def store_rows(ref, value):
    for o in range(ref.shape[0]):
        ref[o] = value[4 * o : 4 * o + 4, :]


def load_rows(ref):
    return jnp.concatenate([ref[o] for o in range(ref.shape[0])], 0)


def solid_tables(k):
    r, c = iota((128, 128), 0), iota((128, 128), 1)
    eye = r == c
    diag = jnp.where(eye, k, 0.0)
    col = jnp.sum(diag, 1, keepdims=True)
    row = jnp.sum(diag, 0, keepdims=True)
    one = jnp.where(eye, 1.0, 0.0)
    s = one - RELAX * k / col
    s2 = mm_full(s, s)
    s4 = mm_full(s2, s2)
    t = mm_full(one + s, one + s2) * (RELAX / row)
    sel = jnp.where((c == 3 * (r & 31) + 2) & ((r & 31) < 27), 1.0, 0.0)
    load = mm_full(t, sel.T)
    top = mm_full(sel, load).T
    return s4, load, top


def strided(ref, a):
    return ref[pl.ds(a, 81, stride=32), :]


def top_sources(wide, disp, modulus, pow_):
    r, c = iota((32, 81), 0), iota((32, 81), 1)
    sel = as_bf16((c == 3 * r + 2) & (r < 27))
    r, c = iota((32, 128), 0), iota((32, 128), 1)
    sel_wide = jnp.where((c == 3 * r + 2) & (r < 27), 1.0, 0.0)
    ph, plo = split(mm_full(sel_wide, pow_)[:, 0:81])
    for k in range(16):
        cols = slice(256 * k, 256 * k + 256)
        d = jnp.concatenate([strided(disp, 2 * k), strided(disp, 2 * k + 1)], 1)
        dh, dl = split(d)
        base = mm(ph, dh) + (mm(ph, dl) + mm(plo, dh))
        inv = jnp.broadcast_to(1.0 / modulus[:, cols], (32, 256))
        bh, bl = split(jnp.where(iota((32, 256), 0) == 27, inv, base))
        wide[0:32, cols] = bh
        wide[32:64, cols] = bl
        wide[64:96, cols] = mm(sel, dh).astype(BF16)
        wide[96:128, cols] = mm(sel, dl).astype(BF16)


def target_row(targets):
    turned = targets.T
    return jnp.concatenate([turned[32 * q : 32 * q + 1, :] for q in range(4)], 1).astype(I32) - 1


def stack_slots(x):
    return jnp.concatenate([x[:, 384 * q : 384 * q + 384] for q in range(4)], 0).T


def gather_top(acc, wide, row):
    high = row >> 7
    low = as_bf16(iota((128, 1536), 0) == (row & 127))
    acc[...] = jnp.zeros((128, 1536), F32)

    def step(i, carry):
        parts = [low * as_bf16(high == 4 * i + j) for j in range(4)]
        one = jnp.concatenate(parts, 0)
        acc[...] += mm(wide[:, pl.ds(pl.multiple_of(512 * i, 512), 512)], one)
        return carry
    lax.fori_loop(0, 8, step, 0)
    base = acc[0:32, :] + acc[32:64, :]
    disp = acc[64:96, :] + acc[96:128, :]
    inv = jnp.broadcast_to(base[27:28, :], (32, 1536))
    return stack_slots(base), stack_slots(disp), stack_slots(inv)


def window_kernel(
    state, speed, metric, face, owner, target, stiff, volume, slope, pick, inject, load,
    disp_any, modulus,
    next_o, wm_o, meta_o, back_o, back0_o, pow_o, load_o, got_o, tgt_o,
    part, fields, u0_s, sx, sy, rx, ry, tgt_s, pay_s, got_t, got_p, rows_s, disp_s, back, back0,
    disp, wide, acc, same, gathered, square,
    hs, hr, bs, br, cs,
):
    grp, gx, gy = lax.axis_index("grp"), lax.axis_index("gx"), lax.axis_index("gy")
    fluid = grp < FLUID
    barrier = pltpu.get_barrier_semaphore()
    column = gx * GY + gy
    has = [gx > 0, gx < GX - 1, gy > 0, gy < GY - 1]
    where = [(grp, gx - 1, gy), (grp, gx + 1, gy), (grp, gx, gy - 1), (grp, gx, gy + 1)]
    owner_group = FLUID + lax.rem(grp, SOLID)
    my_row = (grp // SOLID) * COLS + column

    def halo(stage, k, side):
        buf, into = ((sx, rx), (sy, ry))[k // 2]
        return pltpu.make_async_remote_copy(
            buf.at[stage, k % 2], into.at[stage, side % 2], hs.at[stage, k], hr.at[stage, side],
            **at(*where[k]),
        )

    def start_halos(stage):
        for k in range(4):
            @pl.when(has[k])
            def _():
                halo(stage, k, k ^ 1).start()

    def wait_halos(stage):
        for k in range(4):
            @pl.when(has[k])
            def _():
                halo(stage, k, k).wait_recv()

    def far_faces(stage):
        zero = jnp.zeros((), F32)
        return remote_faces(
            jnp.where(has[0], rx[stage, 0], zero), jnp.where(has[1], rx[stage, 1], zero),
            jnp.where(has[2], ry[stage, 0], zero), jnp.where(has[3], ry[stage, 1], zero),
        )

    def push_to_solid(src, dst, k):
        def push(i, carry):
            o = lax.rem(i + column, COLS)
            pltpu.make_async_remote_copy(
                src.at[o], dst.at[my_row], bs.at[k], br.at[k],
                **at(owner_group, o // GY, lax.rem(o, GY)),
            ).start()
            return carry
        lax.fori_loop(0, COLS, push, 0)

    def push_to_fluid(src, dst, k):
        def push(i, carry):
            level = lax.rem(i, LEVELS)
            c = lax.rem(i // LEVELS + column, COLS)
            pltpu.make_async_remote_copy(
                src.at[level * COLS + c], dst.at[column], bs.at[k], br.at[k],
                **at(level * SOLID + (grp - FLUID), c // GY, lax.rem(c, GY)),
            ).start()
            return carry
        lax.fori_loop(0, LEVELS * COLS, push, 0)

    def whole(ref, k):
        return pltpu.make_async_remote_copy(
            ref, ref, bs.at[k], br.at[k], **at(lax.rem(grp + 1, FLUID + SOLID), gx, gy)
        )

    @pl.when(fluid)
    def _():
        peers = jnp.int32(COLS)
        for k in range(4):
            peers = peers + jnp.where(has[k], 1, 0)

            @pl.when(has[k])
            def _():
                pl.semaphore_signal(barrier, inc=1, **at(*where[k]))

        def greet(i, carry):
            o = lax.rem(i + column, COLS)
            pl.semaphore_signal(barrier, inc=1, **at(owner_group, o // GY, lax.rem(o, GY)))
            return carry
        lax.fori_loop(0, COLS, greet, 0)

        met = flat_metric(metric[...])
        u0 = unpack_nodes(state[...].astype(F32), 4, 250)
        wm = unpack_nodes(speed[...].astype(F32), 3, 256)
        u0_s[...] = u0
        wm_o[...] = wm
        meta = wall_meta(face[...], owner[...])
        meta_o[...] = meta
        plus, minus, _, _ = face_values((pick[...], slope[...]), met, u0, None)
        sx[0, 0], sx[0, 1], sy[0, 0], sy[0, 1] = send_faces(plus, minus)
        store_rows(
            tgt_s, to_slots(meta, jnp.broadcast_to((target[...] + 1).astype(F32), (128, 256)))
        )
        rate = volume_rate(volume[...], met, u0.astype(F32), u0, None, wm)
        faces = local_faces(plus, minus, *open_rows(meta))
        part[...] = rate + inject_faces(inject[...], faces)
        pl.semaphore_wait(barrier, peers)
        start_halos(0)
        push_to_solid(tgt_s, got_t, 0)
        wait_halos(0)

        rate = part[...] + inject_faces(inject[...], far_faces(0))
        v1 = u0_s[...].astype(F32) + DT * rate
        fields[...] = v1
        hi, lo = split(v1)
        plus, minus, s, scaled = face_values((pick[...], slope[...]), met, hi, lo)
        loads = wall_loads(load[...], pick[...], met, s, scaled[2], wm_o[...])
        lh, ll = split(loads)
        hit = as_bf16(iota((512, 256), 0) == face[...])
        rows = mm(lh, hit) + mm(ll, hit)
        store_rows(pay_s, to_slots(meta_o[...], jnp.concatenate([rows] * 4, 0)))
        sx[1, 0], sx[1, 1], sy[1, 0], sy[1, 1] = send_faces(plus, minus)
        push_to_solid(pay_s, got_p, 1)
        start_halos(1)

        faces = local_faces(plus, minus, *open_rows(meta_o[...]))
        rate = volume_rate(volume[...], met, fields[...], hi, lo, wm_o[...])
        part[...] = rate
        wait_halos(1)
        faces = [a + b for a, b in zip(faces[:4], far_faces(1))] + faces[4:]
        rate = part[...] + inject_faces(inject[...], faces)
        result = 0.5 * (u0_s[...].astype(F32) + fields[...]) + (0.5 * DT) * rate
        next_o[...] = result.astype(BF16)
        for stage in range(2):
            for k in range(4):
                @pl.when(has[k])
                def _():
                    halo(stage, k, k ^ 1).wait_send()
        whole(tgt_s, 0).wait_send()
        whole(pay_s, 1).wait_send()
        whole(back0, 2).wait_recv()
        back0_o[...] = load_rows(back0)
        whole(back, 3).wait_recv()
        back_o[...] = load_rows(back)

    @pl.when(jnp.logical_not(fluid))
    def _():
        copy = pltpu.make_async_copy(disp_any, disp, cs)
        copy.start()

        def greet(i, carry):
            g = lax.rem(i, LEVELS) * SOLID + (grp - FLUID)
            c = lax.rem(i // LEVELS + column, COLS)
            pl.semaphore_signal(barrier, inc=1, **at(g, c // GY, lax.rem(c, GY)))
            return carry
        lax.fori_loop(0, LEVELS * COLS, greet, 0)

        r, c = iota((128, 128), 0), iota((128, 128), 1)
        square[...] = jnp.where(r == c, 1.0, 0.0)
        square[0:81, 0:81] = stiff[...]
        pow_, load_t, top = solid_tables(square[...])
        pow_o[...] = pow_
        load_o[...] = load_t
        copy.wait()
        top_sources(wide, disp, modulus, pow_)
        th, tl = split(top)
        pl.semaphore_wait(barrier, LEVELS * COLS)

        whole(got_t, 0).wait_recv()
        targets = load_rows(got_t)
        tgt_o[...] = targets
        row = target_row(targets)
        base, d0, inv = gather_top(acc, wide, row)
        store_rows(disp_s, d0)
        wanted = targets.astype(I32) - 1
        for q in range(4):
            same[384 * q : 384 * q + 384, :] = as_bf16(wanted[:, 32 * q : 32 * q + 1] == row)
        push_to_fluid(disp_s, back0, 2)

        whole(got_p, 1).wait_recv()
        loads = load_rows(got_p)
        got_o[...] = loads
        lane = iota((384, 128), 1)
        for q in range(4):
            h, l = split(jnp.where((lane >> 5) == q, loads, 0.0))
            gathered[384 * q : 384 * q + 384, 0:128] = h
            gathered[384 * q : 384 * q + 384, 128:256] = l
        total = jnp.zeros((384, 128), F32)
        for q in range(4):
            both = mm(same[384 * q : 384 * q + 384, :], gathered[...])
            ah, al = split(both[:, 0:128] + both[:, 128:256])
            res = mm(ah, th) + (mm(al, th) + mm(ah, tl))
            total = jnp.where((lane >> 5) == q, res, total)
        store_rows(rows_s, base + inv * total)
        push_to_fluid(rows_s, back, 3)
        whole(disp_s, 2).wait_send()
        whole(rows_s, 3).wait_send()


def final_kernel(
    dn, d0, meta_r, face, wm, blend, nxt,
    disp_any, modulus, pow_, load, pay, tgt,
    next_o, motion_o, solid_o,
    disp, stage, sem,
):
    r, c = iota((256, 256), 0), iota((256, 256), 1)

    @pl.when(is_fluid())
    def _():
        solid_o[...] = jnp.zeros((2592, 128), F32)
        stage[...] = jnp.zeros((1000, 128), F32)
        result = nxt[...]
        for f in range(4):
            at_row = r - 2 * f
            put = as_bf16(
                (at_row >= 0) & (at_row < 250) & (c == (at_row >> 1) + 128 * (at_row & 1))
            )
            block = result[:, 256 * f : 256 * f + 256]
            pair = jnp.concatenate([block[:, 0:128], block[:, 128:256]], 0)
            stage[248 * f : 248 * f + 256, :] = stage[248 * f : 248 * f + 256, :] + mm(put, pair)
        next_o[...] = stage[...].astype(BF16)

        meta = meta_r[...]
        a = from_slots(meta, dn[...])
        b = from_slots(meta, d0[...])
        hi, lo = split(jnp.concatenate([a, a - b], 0))
        hit = as_bf16(iota((512, 256), 0) == face[...])
        faces = mm_nt(hi, hit) + mm_nt(lo, hit)
        faces = jnp.concatenate([faces[:, 0:256], faces[:, 256:512]], 0)
        hi, lo = split(faces)
        put = as_bf16(c == (r >> 1) + 128 * (r & 1))
        for ch in range(6):
            value = table_times(blend[128 * ch : 128 * ch + 128, :], hi, lo)
            if ch >= 3:
                value = value + wm[:, 256 * (ch - 3) : 256 * (ch - 3) + 256].astype(F32)
            value = value.astype(BF16)
            pair = jnp.concatenate([value[:, 0:128], value[:, 128:256]], 0)
            motion_o[256 * ch : 256 * ch + 256, :] = mm(put, pair).astype(BF16)

    @pl.when(jnp.logical_not(is_fluid()))
    def _():
        copy = pltpu.make_async_copy(disp_any, disp, sem)
        copy.start()
        next_o[...] = jnp.zeros((1000, 128), BF16)
        motion_o[...] = jnp.zeros((1536, 128), BF16)
        row = target_row(tgt[...])
        high = row >> 7
        low = as_bf16(iota((128, 1536), 0) == (row & 127))
        turned = pay[...].T
        wide = jnp.concatenate([turned[32 * q : 32 * q + 32, :] for q in range(4)], 1)
        hi, lo = split(wide)
        th, tl = split(load[...][0:81, 0:32])
        sh, sl = split(pow_[...][0:81, 0:81])
        copy.wait()
        for k in range(8):
            masks = [as_bf16(high == 4 * k + j) for j in range(4)]
            parts = [part * mask for mask in masks for part in (hi, lo)]
            force = mm_nt(jnp.concatenate(parts, 0), low)
            for pair in range(2):
                f = [
                    force[64 * j : 64 * j + 32] + force[64 * j + 32 : 64 * j + 64]
                    for j in (2 * pair, 2 * pair + 1)
                ]
                block = 2 * k + pair
                cols = slice(256 * block, 256 * block + 256)
                fh, fl = split(jnp.concatenate(f, 1) / modulus[:, cols])
                d = jnp.concatenate([strided(disp, 2 * block), strided(disp, 2 * block + 1)], 1)
                dh, dl = split(d)
                out = mm(sh, dh) + (mm(sh, dl) + mm(sl, dh))
                out = out + (mm(th, fh) + (mm(th, fl) + mm(tl, fh)))
                solid_o[pl.ds(2 * block, 81, stride=32), :] = out[:, 0:128]
                solid_o[pl.ds(2 * block + 1, 81, stride=32), :] = out[:, 128:256]


VM = pl.BlockSpec(memory_space=pltpu.VMEM)
ANY = pl.BlockSpec(memory_space=pl.ANY)


def shape(dims, dtype=F32):
    return jax.ShapeDtypeStruct(dims, dtype)


def local(
    fluid_state, mesh_velocity, metric, wall_face, wall_owner, wall_target, solid_disp, modulus,
    stiffness,
):
    tab = {k: jnp.asarray(v) for k, v in build_tables().items()}
    state = fluid_state.reshape(1000, 128)
    speed = jnp.pad(
        mesh_velocity.reshape(3, 125, 2, 128), ((0, 0), (0, 3), (0, 0), (0, 0))
    ).reshape(768, 128)
    met = metric.reshape(3, 2, 128)
    face = wall_face.reshape(1, 256)
    owner = wall_owner.reshape(1, 256)
    target = wall_target.reshape(1, 256)
    disp = solid_disp.reshape(2592, 128)
    mod = modulus.reshape(1, 4096)
    slots = LEVELS * COLS

    nxt, wm, meta, back, back0, pow_, load, got_p, got_t = pl.pallas_call(
        window_kernel,
        out_shape=[
            shape((128, 1024), BF16), shape((128, 768), BF16), shape((8, 256)),
            shape((128, 128)), shape((128, 128)), shape((128, 128)), shape((128, 128)),
            shape((384, 128)), shape((384, 128)),
        ],
        in_specs=[VM] * 12 + [ANY, VM],
        out_specs=[VM] * 9,
        scratch_shapes=[
            pltpu.VMEM((128, 1024), F32), pltpu.VMEM((128, 1024), F32),
            pltpu.VMEM((128, 1024), BF16),
            pltpu.VMEM((2, 2, 32, 1024), F32), pltpu.VMEM((2, 2, 32, 512), F32),
            pltpu.VMEM((2, 2, 32, 1024), F32), pltpu.VMEM((2, 2, 32, 512), F32),
            pltpu.VMEM((COLS, 4, 128), F32), pltpu.VMEM((COLS, 4, 128), F32),
            pltpu.VMEM((slots, 4, 128), F32), pltpu.VMEM((slots, 4, 128), F32),
            pltpu.VMEM((slots, 4, 128), F32), pltpu.VMEM((slots, 4, 128), F32),
            pltpu.VMEM((COLS, 4, 128), F32), pltpu.VMEM((COLS, 4, 128), F32),
            pltpu.VMEM((2592, 128), F32), pltpu.VMEM((128, 4096), BF16),
            pltpu.VMEM((128, 1536), F32), pltpu.VMEM((1536, 1536), BF16),
            pltpu.VMEM((1536, 256), BF16), pltpu.VMEM((128, 128), F32),
            pltpu.SemaphoreType.DMA((2, 4)), pltpu.SemaphoreType.DMA((2, 4)),
            pltpu.SemaphoreType.DMA((4,)), pltpu.SemaphoreType.DMA((4,)),
            pltpu.SemaphoreType.DMA,
        ],
        compiler_params=pltpu.CompilerParams(
            collective_id=0, has_side_effects=True, vmem_limit_bytes=60 * 1024 * 1024
        ),
        name="window",
    )(state, speed, met, face, owner, target, stiffness, tab["volume"], tab["slope"], tab["pick"],
      tab["inject"], tab["load"], disp, mod)

    fluid_next, motion, solid_next = pl.pallas_call(
        final_kernel,
        out_shape=[shape((1000, 128), BF16), shape((1536, 128), BF16), shape((2592, 128))],
        in_specs=[VM] * 7 + [ANY] + [VM] * 5,
        out_specs=[VM] * 3,
        scratch_shapes=[
            pltpu.VMEM((2592, 128), F32), pltpu.VMEM((1000, 128), F32), pltpu.SemaphoreType.DMA,
        ],
        compiler_params=pltpu.CompilerParams(vmem_limit_bytes=60 * 1024 * 1024),
        name="final",
    )(back, back0, meta, face, wm, tab["blend"], nxt, disp, mod, pow_, load, got_p, got_t)

    motion = motion.reshape(6, 128, 2, 128)[:, 0:125]
    return (
        fluid_next.reshape(1, 4, 125, 1, 2, 128),
        motion.reshape(1, 6, 125, 1, 2, 128),
        solid_next.reshape(1, 81, 4096),
    )


def solution(mesh):
    in_specs = (
        P("grp", None, None, "gx", "gy", None),
        P("grp", None, None, "gx", "gy", None),
        P("grp", None, "gx", "gy", None),
        P(("grp", "gx", "gy")),
        P(("grp", "gx", "gy"), None),
        P(("grp", "gx", "gy")),
        P("grp", None, ("gx", "gy")),
        P("grp", ("gx", "gy")),
        P(),
    )
    out_specs = (
        P("grp", None, None, "gx", "gy", None),
        P("grp", None, None, "gx", "gy", None),
        P("grp", None, ("gx", "gy")),
    )
    return jax.shard_map(local, mesh=mesh, in_specs=in_specs, out_specs=out_specs, check_vma=False)
```

```python
import functools
import math

import jax
import jax.numpy as jnp
import numpy as np
from jax import lax
from jax.experimental import pallas as pl
from jax.experimental.pallas import tpu as pltpu
from jax.sharding import PartitionSpec as P

F32 = jnp.float32
BF16 = jnp.bfloat16
I32 = jnp.int32

FLUID = 6
SOLID = 2
LEVELS = 3
GX = 8
GY = 4
COLS = GX * GY
DT = 0.05
NU = 0.02
RELAX = 0.8


def points_5():
    return np.array([-1.0, -math.sqrt(3.0 / 7.0), 0.0, math.sqrt(3.0 / 7.0), 1.0])


def weights_5():
    return np.array([0.1, 49.0 / 90.0, 32.0 / 45.0, 49.0 / 90.0, 0.1])


def lagrange_table(centres, points):
    result = np.ones((len(points), len(centres)))
    for column in range(len(centres)):
        for partner in range(len(centres)):
            if partner != column:
                result[:, column] *= (points - centres[partner]) / (
                    centres[column] - centres[partner]
                )
    return result


def derivative_table():
    pts = points_5()
    n = len(pts)
    w = np.ones(n)
    for c in range(n):
        for p in range(n):
            if p != c:
                w[c] = w[c] / (pts[c] - pts[p])
    d = np.zeros((n, n))
    for r in range(n):
        for c in range(n):
            if r != c:
                d[r, c] = w[c] / w[r] / (pts[r] - pts[c])
        d[r, r] = -np.sum(d[r])
    return d.astype(np.float32).astype(np.float64)


def split_np(x):
    hi = np.asarray(x, np.float32).astype(jnp.bfloat16)
    lo = (np.asarray(x, np.float64) - hi.astype(np.float64)).astype(np.float32).astype(jnp.bfloat16)
    return hi, lo


def build_tables():
    d = derivative_table()
    eye = np.eye(5)
    first = [
        np.kron(np.kron(d, eye), eye),
        np.kron(np.kron(eye, d), eye),
        np.kron(np.kron(eye, eye), d),
    ]
    volume = np.zeros((768, 128))
    for k in range(3):
        volume[128 * k : 128 * k + 125, :125] = first[k]
        volume[384 + 128 * k : 384 + 128 * k + 125, :125] = first[k] @ first[k]
    face_pick = np.zeros((192, 128))
    face_slope = np.zeros((192, 128))
    node = np.arange(125).reshape(5, 5, 5)
    for k in range(3):
        for side in range(2):
            ids = np.take(node, 4 * side, axis=k).reshape(25)
            rows = 64 * k + 32 * side + np.arange(25)
            face_pick[rows, ids] = 1.0
            face_slope[rows, :125] = first[k][ids]
    values = lagrange_table(np.array([-1.0, 0.0, 1.0]), points_5())
    project_one = (values * weights_5()[:, None]).T
    project = np.kron(project_one, project_one).astype(np.float32).astype(np.float64)
    interp = np.kron(values, values).astype(np.float32).astype(np.float64)
    load = np.zeros((32, 96))
    for c in range(3):
        load[9 * c : 9 * c + 9, 32 * c : 32 * c + 25] = project
    blend = np.zeros((768, 128))
    for ch in range(6):
        for nd in range(125):
            ij, k = nd // 5, nd % 5
            for side, scale in ((0, 1.0 - k / 4.0), (1, k / 4.0)):
                base = 64 * side + 32 * (ch // 3) + 9 * (ch % 3)
                blend[128 * ch + nd, base : base + 9] = scale * interp[ij]
    vol_hi, vol_lo = split_np(volume)
    fs_hi, fs_lo = split_np(face_slope)
    load_hi, load_lo = split_np(load)
    blend_hi, blend_lo = split_np(blend)
    return dict(
        volume=np.concatenate([vol_hi, vol_lo], 1),
        slope=np.concatenate([fs_hi, fs_lo], 1),
        pick=face_pick.astype(jnp.bfloat16),
        inject=np.ascontiguousarray(face_pick.T).astype(jnp.bfloat16),
        load=np.concatenate([load_hi, load_lo], 1),
        blend=np.concatenate([blend_hi, blend_lo], 1),
    )


def mm(a, b):
    return jnp.dot(a, b, preferred_element_type=F32)


def mm_nt(a, b):
    return lax.dot_general(a, b, (((1,), (1,)), ((), ())), preferred_element_type=F32)


def mm_full(a, b):
    return jnp.dot(a, b, preferred_element_type=F32, precision=lax.Precision.HIGHEST)


def split(x):
    hi = x.astype(BF16)
    return hi, (x - hi.astype(F32)).astype(BF16)


def iota(shape, axis):
    return lax.broadcasted_iota(I32, shape, axis)


def as_bf16(mask):
    return jnp.where(mask, 1.0, 0.0).astype(BF16)


def table_times(table, hi, lo=None):
    k = table.shape[1] // 2
    out = mm(table, jnp.concatenate([hi, hi], 0))
    if lo is not None:
        out = out + mm(table[:, :k], lo)
    return out


def unpack_nodes(raw, count, stride):
    parts = []
    r, c = iota((256, 256), 0), iota((256, 256), 1)
    y, n = r >> 7, r & 127
    for f in range(count):
        start = stride * f // 8 * 8
        pick = as_bf16((c == stride * f - start + 2 * n + y) & (n < 125))
        window = raw[start : start + 256, :].astype(BF16)
        both = mm(pick, window).astype(BF16)
        parts += [both[0:128, :], both[128:256, :]]
    return jnp.concatenate(parts, 1)


def metric_row(metric, k):
    row = metric[k : k + 1, :]
    return jnp.concatenate([row] * 4, 1)


def face_values(tables, metric, hi, lo):
    pick, slope = tables
    s = mm(pick, hi)
    if lo is not None:
        s = s + mm(pick, lo)
    g = table_times(slope, hi, lo)
    plus, minus, scaled = [], [], []
    for k in range(3):
        m = metric_row(metric, k)
        rows = slice(64 * k, 64 * k + 64)
        mg = m * g[rows]
        a, b = 0.5 * mg, 2.0 * s[rows]
        plus.append(a + b)
        minus.append(a - b)
        scaled.append(mg)
    return plus, minus, s, scaled


def column_blocks(x, y):
    return jnp.concatenate([x[:, 256 * f + 128 * y : 256 * f + 128 * y + 128] for f in range(4)], 1)


def place_blocks(x, y):
    parts = []
    zero = jnp.zeros((x.shape[0], 128), F32)
    for f in range(4):
        pair = [zero, zero]
        pair[y] = x[:, 128 * f : 128 * f + 128]
        parts += pair
    return jnp.concatenate(parts, 1)


def shift_z(x, step):
    blocks = []
    for b in range(x.shape[1] // 128):
        blocks.append(pltpu.roll(x[:, 128 * b : 128 * b + 128], step % 128, 1))
    return jnp.concatenate(blocks, 1)


def local_faces(plus, minus, open_lo, open_hi):
    lo_x, hi_x = minus[0][0:32], -plus[0][32:64]
    in_lo = place_blocks(column_blocks(minus[1][32:64], 0), 1)
    in_hi = place_blocks(column_blocks(plus[1][0:32], 1), 0)
    lo_y, hi_y = minus[1][0:32] - in_lo, in_hi - plus[1][32:64]
    nb_lo = shift_z(minus[2][32:64], 1) * open_lo
    nb_hi = shift_z(plus[2][0:32], -1) * open_hi
    lo_z, hi_z = minus[2][0:32] - nb_lo, nb_hi - plus[2][32:64]
    return [lo_x, hi_x, lo_y, hi_y, lo_z, hi_z]


def send_faces(plus, minus):
    return (
        plus[0][0:32],
        minus[0][32:64],
        column_blocks(plus[1][0:32], 0),
        column_blocks(minus[1][32:64], 1),
    )


def remote_faces(rx_lo, rx_hi, ry_lo, ry_hi):
    return [-rx_lo, rx_hi, place_blocks(-ry_lo, 0), place_blocks(ry_hi, 1)]


def inject_faces(inject, faces):
    hi, lo = split(jnp.concatenate(faces, 0))
    k = hi.shape[0]
    return mm(inject[:, 0:k], hi) + mm(inject[:, 0:k], lo)


def flat_metric(metric):
    return jnp.concatenate([metric[:, 0, :], metric[:, 1, :]], 1)


def open_rows(meta):
    return (
        jnp.concatenate([meta[2:3, 0:256]] * 4, 1),
        jnp.concatenate([meta[3:4, 0:256]] * 4, 1),
    )


def volume_rate(volume, metric, fields, hi, lo, wm):
    blocks = []
    carrier = [
        fields[:, 256 * k : 256 * k + 256] - wm[:, 256 * k : 256 * k + 256].astype(F32)
        for k in range(3)
    ]
    m = [metric[k : k + 1, :] for k in range(3)]
    flow = [carrier[k] * m[k] for k in range(3)]
    curve = [NU * m[k] * m[k] for k in range(3)]
    part_lo = None if lo is None else lo[:, 768:1024]
    press = table_times(volume[0:384], hi[:, 768:1024], part_lo)
    div = None
    for c in range(3):
        cols = slice(256 * c, 256 * c + 256)
        part_lo = None if lo is None else lo[:, cols]
        der = table_times(volume, hi[:, cols], part_lo)
        rate = -m[c] * press[128 * c : 128 * c + 128]
        for k in range(3):
            rate = rate + curve[k] * der[384 + 128 * k : 512 + 128 * k]
            rate = rate - flow[k] * der[128 * k : 128 * k + 128]
        own = m[c] * der[128 * c : 128 * c + 128]
        div = own if div is None else div + own
        blocks.append(rate)
    blocks.append(-div)
    return jnp.concatenate(blocks, 1)


def wall_meta(face, owner):
    d = as_bf16(iota((32, 256), 0) == owner)
    before = as_bf16(iota((256, 256), 0) < iota((256, 256), 1))
    count = mm(d, before)
    slot = jnp.sum(jnp.where(iota((32, 256), 0) == owner, count, 0.0), 0, keepdims=True).astype(I32)
    hit = as_bf16(iota((512, 256), 0) == face)
    walled = mm_nt(jnp.ones((8, 256), BF16), hit)[0:1, :]
    z = iota((1, 256), 1) & 127
    open_lo = jnp.where(z == 0, 0.0, 1.0 - walled[:, 0:256])
    open_hi = jnp.where(z == 127, 0.0, 1.0 - walled[:, 256:512])
    row0 = (owner * 4 + (slot >> 2)).astype(F32)
    row1 = (slot & 3).astype(F32)
    return jnp.concatenate([row0, row1, open_lo, open_hi, jnp.zeros((4, 256), F32)], 0)


def slot_matrix(meta):
    return as_bf16(iota((128, 256), 0) == meta[0:1, :].astype(I32))


def quarter_mask(meta):
    return (iota((128, 256), 0) >> 5) == meta[1:2, :].astype(I32)


def to_slots(meta, rows):
    hi, lo = split(jnp.where(quarter_mask(meta), rows, 0.0))
    a = slot_matrix(meta)
    return mm_nt(a, hi) + mm_nt(a, lo)


def from_slots(meta, packed):
    hi, lo = split(packed.T)
    a = slot_matrix(meta)
    wide = jnp.where(quarter_mask(meta), mm(hi, a) + mm(lo, a), 0.0)
    return (wide[0:32] + wide[32:64]) + (wide[64:96] + wide[96:128])


def wall_loads(load, pick, metric, s, scaled_z, wm):
    wz = mm(pick[128:192], wm[:, 512:768])
    out = []
    for side, sign in ((0, -1.0), (1, 1.0)):
        g = scaled_z[32 * side : 32 * side + 32]
        v = s[128 + 32 * side : 160 + 32 * side]
        parts = [0.2 * sign * g[:, 0:256], 0.2 * sign * g[:, 256:512]]
        w = wz[32 * side : 32 * side + 32]
        parts.append(
            sign * (0.2 * g[:, 512:768] - v[:, 768:1024] + 0.5 * (v[:, 512:768] - w))
        )
        hi, lo = split(jnp.concatenate(parts, 0))
        out.append(table_times(load, hi, lo))
    return jnp.concatenate(out, 1)


MESH = pl.DeviceIdType.MESH


def is_fluid():
    return lax.axis_index("grp") < FLUID


def at(grp, gx, gy):
    return dict(device_id=(grp, gx, gy), device_id_type=MESH)


def store_rows(ref, value):
    for o in range(ref.shape[0]):
        ref[o] = value[4 * o : 4 * o + 4, :]


def load_rows(ref):
    return jnp.concatenate([ref[o] for o in range(ref.shape[0])], 0)


def solid_tables(k):
    r, c = iota((128, 128), 0), iota((128, 128), 1)
    eye = r == c
    diag = jnp.where(eye, k, 0.0)
    col = jnp.sum(diag, 1, keepdims=True)
    row = jnp.sum(diag, 0, keepdims=True)
    one = jnp.where(eye, 1.0, 0.0)
    s = one - RELAX * k / col
    s2 = mm_full(s, s)
    s4 = mm_full(s2, s2)
    t = mm_full(one + s, one + s2) * (RELAX / row)
    sel = jnp.where((c == 3 * (r & 31) + 2) & ((r & 31) < 27), 1.0, 0.0)
    load = mm_full(t, sel.T)
    top = mm_full(sel[0:32], load)[:, 0:32]
    return s4, load, top


def pack_pairs(stage, f, pair):
    start = 250 * f // 8 * 8
    r, c = iota((256, 256), 0), iota((256, 256), 1)
    at_row = r - (250 * f - start)
    put = as_bf16((at_row >= 0) & (at_row < 250) & (c == (at_row >> 1) + 128 * (at_row & 1)))
    value = mm(put, pair)
    if 250 * f % 8:
        stage[start : start + 8, :] = stage[start : start + 8, :] + value[0:8]
        stage[start + 8 : start + 256, :] = value[8:256]
    else:
        stage[start : start + 256, :] = value


def strided(ref, a):
    return ref[pl.ds(a, 81, stride=32), :]


def power_sources(keep, wide, disp, modulus, pow_):
    r, c = iota((32, 81), 0), iota((32, 81), 1)
    sel = as_bf16((c == 3 * r + 2) & (r < 27))
    ph, plo = split(pow_[0:81, 0:81])
    for k in range(16):
        cols = slice(256 * k, 256 * k + 256)
        d = jnp.concatenate([strided(disp, 2 * k), strided(disp, 2 * k + 1)], 1)
        dh, dl = split(d)
        value = mm(ph, dh) + (mm(ph, dl) + mm(plo, dh))
        keep[:, cols] = value
        kh, kl = split(value)
        inv_h, inv_l = split(jnp.broadcast_to(1.0 / modulus[:, cols], (32, 256)))
        spare = iota((32, 256), 0) == 27
        wide[0:32, cols] = jnp.where(spare, inv_h.astype(F32), mm(sel, kh)).astype(BF16)
        wide[32:64, cols] = jnp.where(spare, inv_l.astype(F32), mm(sel, kl)).astype(BF16)
        wide[64:96, cols] = mm(sel, dh).astype(BF16)
        wide[96:128, cols] = mm(sel, dl).astype(BF16)


def target_row(targets):
    turned = targets.T
    return jnp.concatenate([turned[32 * q : 32 * q + 1, :] for q in range(4)], 1).astype(I32) - 1


def stack_slots(x):
    return jnp.concatenate([x[:, 384 * q : 384 * q + 384] for q in range(4)], 0).T


def gather_top(acc, wide, row):
    high = row >> 7
    low = as_bf16(iota((128, 1536), 0) == (row & 127))
    acc[...] = jnp.zeros((128, 1536), F32)

    def step(i, carry):
        parts = [low * as_bf16(high == 4 * i + j) for j in range(4)]
        one = jnp.concatenate(parts, 0)
        acc[...] += mm(wide[:, pl.ds(pl.multiple_of(512 * i, 512), 512)], one)
        return carry
    lax.fori_loop(0, 8, step, 0)
    return acc[0:32, :] + acc[32:64, :], acc[64:96, :] + acc[96:128, :]


def window_kernel(
    state, speed, metric, face, owner, target, stiff, volume, slope, pick, inject, load,
    disp_any, modulus,
    next_o, wm_o, meta_o, back_o, back0_o, solid_o,
    part, fields, u0_s, sx, sy, rx, ry, tgt_s, pay_s, got_t, got_p, rows_s, disp_s, back, back0,
    disp, wide, acc, same, keep, square, raw, stage_s,
    hs, hr, bs, br, cs,
):
    grp, gx, gy = lax.axis_index("grp"), lax.axis_index("gx"), lax.axis_index("gy")
    fluid = grp < FLUID
    barrier = pltpu.get_barrier_semaphore()
    column = gx * GY + gy
    has = [gx > 0, gx < GX - 1, gy > 0, gy < GY - 1]
    where = [(grp, gx - 1, gy), (grp, gx + 1, gy), (grp, gx, gy - 1), (grp, gx, gy + 1)]
    owner_group = FLUID + lax.rem(grp, SOLID)
    my_row = (grp // SOLID) * COLS + column

    def halo(stage, k, side):
        buf, into = ((sx, rx), (sy, ry))[k // 2]
        return pltpu.make_async_remote_copy(
            buf.at[stage, k % 2], into.at[stage, side % 2], hs.at[stage, k], hr.at[stage, side],
            **at(*where[k]),
        )

    def start_halos(stage):
        for k in range(4):
            @pl.when(has[k])
            def _():
                halo(stage, k, k ^ 1).start()

    def wait_halos(stage):
        for k in range(4):
            @pl.when(has[k])
            def _():
                halo(stage, k, k).wait_recv()

    def far_faces(stage):
        zero = jnp.zeros((), F32)
        return remote_faces(
            jnp.where(has[0], rx[stage, 0], zero), jnp.where(has[1], rx[stage, 1], zero),
            jnp.where(has[2], ry[stage, 0], zero), jnp.where(has[3], ry[stage, 1], zero),
        )

    others = [lax.rem(gy + b, GY) for b in range(GY)]

    def push_to_solid(src, dst, k):
        def push(i, carry):
            x = lax.rem(gx + i, GX)
            for y in others:
                pltpu.make_async_remote_copy(
                    src.at[x * GY + y], dst.at[my_row], bs.at[k], br.at[k], **at(owner_group, x, y)
                ).start()
            return carry
        lax.fori_loop(0, GX, push, 0)

    def push_to_fluid(src, dst, k):
        def push(i, carry):
            x = lax.rem(gx + i, GX)
            for level in range(LEVELS):
                for y in others:
                    pltpu.make_async_remote_copy(
                        src.at[level * COLS + x * GY + y], dst.at[column], bs.at[k], br.at[k],
                        **at(level * SOLID + (grp - FLUID), x, y),
                    ).start()
            return carry
        lax.fori_loop(0, GX, push, 0)

    def whole(ref, k):
        return pltpu.make_async_remote_copy(
            ref, ref, bs.at[k], br.at[k], **at(lax.rem(grp + 1, FLUID + SOLID), gx, gy)
        )

    @pl.when(fluid)
    def _():
        peers = jnp.int32(COLS)
        for k in range(4):
            peers = peers + jnp.where(has[k], 1, 0)

            @pl.when(has[k])
            def _():
                pl.semaphore_signal(barrier, inc=1, **at(*where[k]))

        def greet(i, carry):
            x = lax.rem(gx + i, GX)
            for y in others:
                pl.semaphore_signal(barrier, inc=1, **at(owner_group, x, y))
            return carry
        lax.fori_loop(0, GX, greet, 0)

        met = flat_metric(metric[...])
        u0 = unpack_nodes(state[...].astype(F32), 4, 250)
        raw[744:752, :] = jnp.zeros((8, 128), F32)
        for i in range(375):
            raw[2 * i : 2 * i + 2, :] = speed[i].astype(F32)
        wm = unpack_nodes(raw[...], 3, 250)
        u0_s[...] = u0
        wm_o[...] = wm
        meta = wall_meta(face[...], owner[...])
        meta_o[...] = meta
        plus, minus, _, _ = face_values((pick[...], slope[...]), met, u0, None)
        sx[0, 0], sx[0, 1], sy[0, 0], sy[0, 1] = send_faces(plus, minus)
        store_rows(
            tgt_s, to_slots(meta, jnp.broadcast_to((target[...] + 1).astype(F32), (128, 256)))
        )
        rate = volume_rate(volume[...], met, u0.astype(F32), u0, None, wm)
        faces = local_faces(plus, minus, *open_rows(meta))
        part[...] = rate + inject_faces(inject[...], faces)
        pl.semaphore_wait(barrier, peers)
        start_halos(0)
        push_to_solid(tgt_s, got_t, 0)
        wait_halos(0)

        rate = part[...] + inject_faces(inject[...], far_faces(0))
        v1 = u0_s[...].astype(F32) + DT * rate
        fields[...] = v1
        hi, lo = split(v1)
        plus, minus, s, scaled = face_values((pick[...], slope[...]), met, hi, lo)
        loads = wall_loads(load[...], pick[...], met, s, scaled[2], wm_o[...])
        lh, ll = split(loads)
        hit = as_bf16(iota((512, 256), 0) == face[...])
        rows = mm(lh, hit) + mm(ll, hit)
        store_rows(pay_s, to_slots(meta_o[...], jnp.concatenate([rows] * 4, 0)))
        sx[1, 0], sx[1, 1], sy[1, 0], sy[1, 1] = send_faces(plus, minus)
        push_to_solid(pay_s, got_p, 1)
        start_halos(1)

        faces = local_faces(plus, minus, *open_rows(meta_o[...]))
        rate = volume_rate(volume[...], met, fields[...], hi, lo, wm_o[...])
        part[...] = rate
        wait_halos(1)
        faces = [a + b for a, b in zip(faces[:4], far_faces(1))] + faces[4:]
        rate = part[...] + inject_faces(inject[...], faces)
        result = 0.5 * (u0_s[...].astype(F32) + fields[...]) + (0.5 * DT) * rate
        result = result.astype(BF16)
        for f in range(4):
            block = result[:, 256 * f : 256 * f + 256]
            pack_pairs(stage_s, f, jnp.concatenate([block[:, 0:128], block[:, 128:256]], 0))
        next_o[...] = stage_s[...].astype(BF16)
        for stage in range(2):
            for k in range(4):
                @pl.when(has[k])
                def _():
                    halo(stage, k, k ^ 1).wait_send()
        whole(tgt_s, 0).wait_send()
        whole(pay_s, 1).wait_send()
        whole(back0, 2).wait_recv()
        back0_o[...] = load_rows(back0)
        whole(back, 3).wait_recv()
        back_o[...] = load_rows(back)

    @pl.when(jnp.logical_not(fluid))
    def _():
        copy = pltpu.make_async_copy(disp_any, disp, cs)
        copy.start()

        def greet(i, carry):
            x = lax.rem(gx + i, GX)
            for level in range(LEVELS):
                for y in others:
                    pl.semaphore_signal(barrier, inc=1, **at(level * SOLID + (grp - FLUID), x, y))
            return carry
        lax.fori_loop(0, GX, greet, 0)

        r, c = iota((128, 128), 0), iota((128, 128), 1)
        square[...] = jnp.where(r == c, 1.0, 0.0)
        square[0:81, 0:81] = stiff[...]
        pow_, load_t, top = solid_tables(square[...])
        copy.wait()
        power_sources(keep, wide, disp, modulus, pow_)
        th, tl = split(top)
        pl.semaphore_wait(barrier, LEVELS * COLS)

        whole(got_t, 0).wait_recv()
        targets = load_rows(got_t)
        row = target_row(targets)
        base, d0 = gather_top(acc, wide, row)
        store_rows(disp_s, stack_slots(d0))
        push_to_fluid(disp_s, back0, 2)
        wanted = targets.astype(I32) - 1
        for q in range(4):
            same[384 * q : 384 * q + 384, :] = as_bf16(wanted[:, 32 * q : 32 * q + 1] == row)

        whole(got_p, 1).wait_recv()
        turned = load_rows(got_p).T
        loads = jnp.concatenate([turned[32 * q : 32 * q + 32, :] for q in range(4)], 1)
        hi, lo = split(loads)
        both = mm(jnp.concatenate([hi, lo], 0), same[...])
        fh, fl = split(both[0:32] + both[32:64])
        total = mm(th, fh) + (mm(tl, fh) + mm(th, fl))
        store_rows(rows_s, stack_slots(base + base[27:28, :] * total))
        push_to_fluid(rows_s, back, 3)

        high = row >> 7
        low = as_bf16(iota((128, 1536), 0) == (row & 127))
        lh, ll = split(load_t[0:81, 0:32])
        for k in range(8):
            masks = [as_bf16(high == 4 * k + j) for j in range(4)]
            parts = [part * mask for mask in masks for part in (hi, lo)]
            force = mm_nt(jnp.concatenate(parts, 0), low)
            for pair in range(2):
                f = [
                    force[64 * j : 64 * j + 32] + force[64 * j + 32 : 64 * j + 64]
                    for j in (2 * pair, 2 * pair + 1)
                ]
                block = 2 * k + pair
                cols = slice(256 * block, 256 * block + 256)
                fh, fl = split(jnp.concatenate(f, 1) / modulus[:, cols])
                out = keep[:, cols] + (mm(lh, fh) + (mm(lh, fl) + mm(ll, fh)))
                disp[pl.ds(2 * block, 81, stride=32), :] = out[:, 0:128]
                disp[pl.ds(2 * block + 1, 81, stride=32), :] = out[:, 128:256]
        copy = pltpu.make_async_copy(disp, solid_o, cs)
        copy.start()
        copy.wait()
        whole(disp_s, 2).wait_send()
        whole(rows_s, 3).wait_send()


def final_kernel(
    dn, d0, meta_r, face, wm, blend, next_any, solid_any,
    next_o, motion_o, solid_o,
    moved, kept, stage, sems,
):
    parts = 4
    size = 2592 // parts
    next_in = pltpu.make_async_copy(next_any, kept, sems.at[0])
    next_out = pltpu.make_async_copy(kept, next_o, sems.at[1])
    ins = [
        pltpu.make_async_copy(
            solid_any.at[pl.ds(size * i, size)], moved.at[pl.ds(size * i, size)], sems.at[2 + i]
        )
        for i in range(parts)
    ]
    outs = [
        pltpu.make_async_copy(
            moved.at[pl.ds(size * i, size)], solid_o.at[pl.ds(size * i, size)], sems.at[6 + i]
        )
        for i in range(parts)
    ]

    @pl.when(is_fluid())
    def _():
        next_in.start()
        moved[...] = jnp.zeros((2592, 128), F32)
        for copy in outs:
            copy.start()
        meta = meta_r[...]
        a = from_slots(meta, dn[...])
        b = from_slots(meta, d0[...])
        hi, lo = split(jnp.concatenate([a, a - b], 0))
        hit = as_bf16(iota((512, 256), 0) == face[...])
        faces = mm_nt(hi, hit) + mm_nt(lo, hit)
        faces = jnp.concatenate([faces[:, 0:256], faces[:, 256:512]], 0)
        hi, lo = split(faces)
        next_in.wait()
        next_out.start()
        for ch in range(6):
            value = table_times(blend[128 * ch : 128 * ch + 128, :], hi, lo)
            if ch >= 3:
                value = value + wm[:, 256 * (ch - 3) : 256 * (ch - 3) + 256].astype(F32)
            value = value.astype(BF16)
            pack_pairs(stage, ch, jnp.concatenate([value[:, 0:128], value[:, 128:256]], 0))
        for i in range(375):
            motion_o[i] = stage[4 * i : 4 * i + 4, :].astype(BF16)
        for copy in outs:
            copy.wait()
        next_out.wait()

    @pl.when(jnp.logical_not(is_fluid()))
    def _():
        for copy in ins:
            copy.start()
        kept[...] = jnp.zeros((1000, 128), BF16)
        next_out.start()
        motion_o[...] = jnp.zeros((375, 4, 128), BF16)
        for i in range(parts):
            ins[i].wait()
            outs[i].start()
        for copy in outs:
            copy.wait()
        next_out.wait()


VM = pl.BlockSpec(memory_space=pltpu.VMEM)
ANY = pl.BlockSpec(memory_space=pl.ANY)


def shape(dims, dtype=F32):
    return jax.ShapeDtypeStruct(dims, dtype)


def local(
    fluid_state, mesh_velocity, metric, wall_face, wall_owner, wall_target, solid_disp, modulus,
    stiffness,
):
    tab = {k: jnp.asarray(v) for k, v in build_tables().items()}
    state = fluid_state.reshape(1000, 128)
    speed = mesh_velocity.reshape(375, 2, 128)
    met = metric.reshape(3, 2, 128)
    face = wall_face.reshape(1, 256)
    owner = wall_owner.reshape(1, 256)
    target = wall_target.reshape(1, 256)
    disp = solid_disp.reshape(2592, 128)
    mod = modulus.reshape(1, 4096)
    slots = LEVELS * COLS

    nxt, wm, meta, back, back0, moved = pl.pallas_call(
        window_kernel,
        out_shape=[
            shape((1000, 128), BF16), shape((128, 768), BF16), shape((8, 256)),
            shape((128, 128)), shape((128, 128)), shape((2592, 128)),
        ],
        in_specs=[VM] * 12 + [ANY, VM],
        out_specs=[VM] * 5 + [ANY],
        scratch_shapes=[
            pltpu.VMEM((128, 1024), F32), pltpu.VMEM((128, 1024), F32),
            pltpu.VMEM((128, 1024), BF16),
            pltpu.VMEM((2, 2, 32, 1024), F32), pltpu.VMEM((2, 2, 32, 512), F32),
            pltpu.VMEM((2, 2, 32, 1024), F32), pltpu.VMEM((2, 2, 32, 512), F32),
            pltpu.VMEM((COLS, 4, 128), F32), pltpu.VMEM((COLS, 4, 128), F32),
            pltpu.VMEM((slots, 4, 128), F32), pltpu.VMEM((slots, 4, 128), F32),
            pltpu.VMEM((slots, 4, 128), F32), pltpu.VMEM((slots, 4, 128), F32),
            pltpu.VMEM((COLS, 4, 128), F32), pltpu.VMEM((COLS, 4, 128), F32),
            pltpu.VMEM((2592, 128), F32), pltpu.VMEM((128, 4096), BF16),
            pltpu.VMEM((128, 1536), F32), pltpu.VMEM((1536, 1536), BF16),
            pltpu.VMEM((81, 4096), F32), pltpu.VMEM((128, 128), F32),
            pltpu.VMEM((752, 128), F32), pltpu.VMEM((1000, 128), F32),
            pltpu.SemaphoreType.DMA((2, 4)), pltpu.SemaphoreType.DMA((2, 4)),
            pltpu.SemaphoreType.DMA((4,)), pltpu.SemaphoreType.DMA((4,)),
            pltpu.SemaphoreType.DMA,
        ],
        compiler_params=pltpu.CompilerParams(
            collective_id=0, has_side_effects=True, vmem_limit_bytes=60 * 1024 * 1024
        ),
        name="window",
    )(state, speed, met, face, owner, target, stiffness, tab["volume"], tab["slope"], tab["pick"],
      tab["inject"], tab["load"], disp, mod)

    fluid_next, motion, solid_next = pl.pallas_call(
        final_kernel,
        out_shape=[shape((1000, 128), BF16), shape((375, 4, 128), BF16), shape((2592, 128))],
        in_specs=[VM] * 6 + [ANY] * 2,
        out_specs=[ANY, VM, ANY],
        scratch_shapes=[
            pltpu.VMEM((2592, 128), F32), pltpu.VMEM((1000, 128), BF16),
            pltpu.VMEM((1512, 128), F32), pltpu.SemaphoreType.DMA((10,)),
        ],
        compiler_params=pltpu.CompilerParams(vmem_limit_bytes=60 * 1024 * 1024),
        name="final",
    )(back, back0, meta, face, wm, tab["blend"], nxt, moved)

    return (
        fluid_next.reshape(1, 4, 125, 1, 2, 128),
        motion.reshape(1, 6, 125, 1, 2, 128),
        solid_next.reshape(1, 81, 4096),
    )


def solution(mesh):
    in_specs = (
        P("grp", None, None, "gx", "gy", None),
        P("grp", None, None, "gx", "gy", None),
        P("grp", None, "gx", "gy", None),
        P(("grp", "gx", "gy")),
        P(("grp", "gx", "gy"), None),
        P(("grp", "gx", "gy")),
        P("grp", None, ("gx", "gy")),
        P("grp", ("gx", "gy")),
        P(),
    )
    out_specs = (
        P("grp", None, None, "gx", "gy", None),
        P("grp", None, None, "gx", "gy", None),
        P("grp", None, ("gx", "gy")),
    )
    return jax.shard_map(local, mesh=mesh, in_specs=in_specs, out_specs=out_specs, check_vma=False)
```
